32 devices in a mesh: group: 4 (over y, core), member: 8 (over z, x).
Axes of the slice: x: 2, y: 2, z: 4, core: 2. Of those that a mesh axis runs over, the one named last changes fastest.
Arguments:
- features: bfloat16 [16384, 128], P(('group', 'member')), may hold values from -6 to 6
- edge_tiles: bfloat16 [8192, 128, 128], P(('group', 'member')), may hold values from -0.09375 to 0.09375
- tile_slot: int32 [32, 256], P(('group', 'member')), may hold values from 0 to 7
- tile_column: int32 [32, 256], P(('group', 'member')), may hold values from 0 to 31
- mirror_count: int32 [32, 4], P(('group', 'member')), may hold values from 0 to 2, as said below
- mirror_block: int32 [32, 4, 2], P(('group', 'member')), may hold values from 0 to 3, as said below
- weight_first: bfloat16 [128, 256], replicated, may hold values from -0.5 to 0.5
- bias_first: float32 [256], replicated, may hold values from -3 to 3
- weight_second: bfloat16 [256, 256], replicated, may hold values from -0.375 to 0.375
- bias_second: float32 [256], replicated, may hold values from -3 to 3
Outputs:
- layer_out: bfloat16 [16384, 256], P(('group', 'member'))
The draws below stay inside these ranges and needn't reach their ends.
Inputs may be any that keep to these rules, and one draw needn't show every extreme that they name: `mirror_count`: at most 2 live mirror slots of one device for one destination group. `mirror_block`: the 2 entries of one device and destination group are distinct.
All inputs are finite; a program needn't handle non-finite values.
Results may differ from the reference program's by a relative error of at most 0.01.
Values may be sent and summed in bfloat16 or wider, within the bound.
A program may use at most 64 MiB of HBM per device.

```python
import jax
import jax.numpy as jnp
from jax import lax

TILE = 128
F_IN = 128
HID = 256
BLK_DEV = 4
TILES_DEV = 256
SLOT_CAP = 2
NODES = 16384
DEVICES_ALL = 32
N_GROUP = 4
N_MEMBER = 8


def draw_mirror_count(key, part):
    device_total = N_GROUP * N_MEMBER
    extra = jax.random.randint(key, (device_total, N_GROUP), 0, SLOT_CAP + 1)
    first = (jnp.arange(N_GROUP) == 0)[None, :]
    return jnp.where(first, SLOT_CAP, extra).astype(jnp.int32)


def draw_mirror_block(key, part):
    device_total = N_GROUP * N_MEMBER
    scores = jax.random.randint(key, (device_total, N_GROUP, BLK_DEV), 0, 1048576)
    scores = scores * BLK_DEV + jnp.arange(BLK_DEV)[None, None, :]
    order = jnp.argsort(scores, axis=-1)
    return order[:, :, :SLOT_CAP].astype(jnp.int32)


def with_ends(drawn, own_key, smallest, largest):
    dims = drawn.shape
    index_at = [jax.random.randint(jax.random.fold_in(own_key, axis), (), 0, dims[axis]) for axis in range(len(dims))]
    drawn = drawn.at[tuple(index_at)].set(smallest)
    longest = dims.index(max(dims))
    index_at[longest] = (index_at[longest] + 1) % dims[longest]
    return drawn.at[tuple(index_at)].set(largest)


def level_of(key, extent, split, low, largest):
    def one(axis_at, blocks):
        heights = jax.random.uniform(jax.random.fold_in(jax.random.fold_in(key, 6), axis_at), (blocks,), jnp.float32, low / len(split), largest / len(split))
        return jnp.repeat(jnp.exp(heights), extent[axis_at] // blocks).reshape((-1,) + (1,) * (len(extent) - axis_at - 1))

    level = one(*split[0])
    for cut in split[1:]:
        level = level * one(*cut)
    return level


def scatter_about(own_key, extent, width, bound, shards=(), kind=jnp.bfloat16):
    gain = level_of(own_key, extent, shards, -0.22, 0.18) if shards else 1.0
    values = jax.random.normal(own_key, extent, jnp.float32) * width * gain
    return jnp.minimum(jnp.maximum(values, -bound), bound).astype(kind)


def setup_inputs(seed: int = 0) -> dict:
    splits = jax.random.split(jax.random.key(seed), 11)
    features = scatter_about(splits[0], (NODES, F_IN), 1.0, 6.0, ((0, 32),))
    edge_tiles = scatter_about(splits[1], (DEVICES_ALL * TILES_DEV, TILE, TILE), (TILE * TILES_DEV // 8) ** -0.5, 0.09375, ((0, 32),))
    tile_slot = with_ends(jax.random.randint(splits[2], (DEVICES_ALL, TILES_DEV), 0, N_GROUP * SLOT_CAP), jax.random.fold_in(splits[2], 1), 0, (N_GROUP * SLOT_CAP) - 1).astype(jnp.int32)
    tile_column = with_ends(jax.random.randint(splits[3], (DEVICES_ALL, TILES_DEV), 0, N_MEMBER * BLK_DEV), jax.random.fold_in(splits[3], 1), 0, (N_MEMBER * BLK_DEV) - 1).astype(jnp.int32)
    mirror_count = draw_mirror_count(jax.random.fold_in(splits[10], 71), 0)
    mirror_block = draw_mirror_block(jax.random.fold_in(splits[10], 71), 0)
    weight_first = scatter_about(splits[6], (F_IN, HID), F_IN ** -0.5, 0.5)
    bias_first = scatter_about(splits[7], (HID,), 0.5, 3.0, (), jnp.float32)
    weight_second = scatter_about(splits[8], (HID, HID), HID ** -0.5, 0.375)
    bias_second = scatter_about(splits[9], (HID,), 0.5, 3.0, (), jnp.float32)
    return dict(features=features, edge_tiles=edge_tiles, tile_slot=tile_slot, tile_column=tile_column, mirror_count=mirror_count, mirror_block=mirror_block, weight_first=weight_first, bias_first=bias_first, weight_second=weight_second, bias_second=bias_second)


def reference(features, edge_tiles, tile_slot, tile_column, mirror_count, mirror_block, weight_first, bias_first, weight_second, bias_second):
    device_total = N_GROUP * N_MEMBER
    slot_total = N_GROUP * SLOT_CAP
    device_ids = jnp.arange(device_total, dtype=jnp.int32)
    group_index = device_ids // N_MEMBER
    member_index = device_ids % N_MEMBER
    dest_group = (tile_slot // SLOT_CAP).astype(jnp.int32)
    within = (tile_slot % SLOT_CAP).astype(jnp.int32)
    slot_count = jnp.take_along_axis(mirror_count, dest_group, axis=1)
    alive_mask = (within < slot_count).astype(jnp.float32)
    sources = (group_index[:, None] * (N_MEMBER * BLK_DEV) + tile_column).astype(jnp.int32)
    slot_group = (jnp.arange(slot_total, dtype=jnp.int32) // SLOT_CAP).astype(jnp.int32)
    slot_targets = ((slot_group[None, :] * N_MEMBER + member_index[:, None]) * BLK_DEV + mirror_block.reshape(device_total, slot_total)).astype(jnp.int32)
    tile_grid = edge_tiles.reshape(device_total, TILES_DEV, TILE, TILE)

    def aggregate(node_rows):
        channels = node_rows.shape[1]
        block_rows = node_rows.reshape(-1, TILE, channels).astype(jnp.float32)

        def advance(totals, pieces):
            tile_set, slot_set, source_set, alive_set, target_set = pieces
            products = jnp.einsum("tij,tjf->tif", tile_set.astype(jnp.float32), block_rows[source_set], precision=lax.Precision.HIGHEST)
            products = products * alive_set[:, None, None]
            partial_value = jnp.zeros((slot_total, TILE, channels), jnp.float32).at[slot_set].add(products)
            partial_value = lax.optimization_barrier(partial_value.astype(jnp.bfloat16)).astype(jnp.float32)
            return totals.at[target_set].add(partial_value), None

        start = jnp.zeros(block_rows.shape, jnp.float32)
        totals, _ = lax.scan(advance, start, (tile_grid, tile_slot.astype(jnp.int32), sources, alive_mask, slot_targets))
        return totals.reshape(-1, channels)

    first_sum = aggregate(features).astype(jnp.bfloat16)
    hidden = jnp.maximum(jnp.dot(first_sum, weight_first, preferred_element_type=jnp.float32) + bias_first, 0.0).astype(jnp.bfloat16)
    second = aggregate(hidden).astype(jnp.bfloat16)
    return (jnp.dot(second, weight_second, preferred_element_type=jnp.float32) + bias_second).astype(jnp.bfloat16)
```

```python
import functools

import jax
import jax.numpy as jnp
from jax import lax
from jax.experimental import pallas as pl
from jax.experimental.pallas import tpu as pltpu
from jax.sharding import PartitionSpec as P

F32 = jnp.float32
BF16 = jnp.bfloat16


def general_kernel(
    outer,
    inner,
    groups,
    cap,
    keep,
    slot_ref,
    column_ref,
    count_ref,
    mirror_ref,
    feat_ref,
    tiles_ref,
    w1_ref,
    b1_ref,
    w2_ref,
    b2_ref,
    out_ref,
    tile_buf,
    run_buf,
    stage_buf,
    gather1,
    gather2,
    acc1,
    acc2,
    part1,
    part2,
    got1,
    got2,
    got_hot,
    own_sum,
    hot_ref,
    prev_vmem,
    last_vmem,
    prev_ref,
    last_ref,
    table_sem,
    tile_sem,
    hot_send,
    hot_recv,
    ag1_send,
    ag1_recv,
    rs1_send,
    rs1_recv,
    ag2_send,
    ag2_recv,
    rs2_send,
    rs2_recv,
):
    n = outer * inner
    me = lax.axis_index("member")
    me_outer, me_inner = me // inner, lax.rem(me, inner)
    g = lax.axis_index("group")
    total = tiles_ref.shape[0]
    size = tiles_ref.shape[1]
    rows = feat_ref.shape[0]
    blocks = rows // size
    slots = groups * cap
    columns = n * blocks
    pieces = tile_sem.shape[0]
    piece = total // pieces

    def tile_copy(i):
        span = pl.ds(i * piece, piece)
        return pltpu.make_async_copy(tiles_ref.at[span], tile_buf.at[span], tile_sem.at[i])

    def outer_copy(src, bank, j, send, recv, arriving=False):
        from_outer = lax.rem(me_outer + outer - j, outer)
        origin = from_outer * inner + me_inner
        to = lax.rem(me_outer + j, outer) * inner + me_inner
        return pltpu.make_async_remote_copy(
            src_ref=src,
            dst_ref=bank.at[origin if arriving else me],
            send_sem=send.at[j],
            recv_sem=recv.at[j],
            device_id={"member": to},
            device_id_type=pl.DeviceIdType.MESH,
        )

    def inner_copy(src, bank, j, hop, send, recv, arriving=False):
        from_outer = lax.rem(me_outer + outer - j, outer)
        from_inner = lax.rem(me_inner + inner - hop, inner)
        mine = from_outer * inner + me_inner
        origin = from_outer * inner + from_inner
        to = me_outer * inner + lax.rem(me_inner + hop, inner)
        at = outer + j * (inner - 1) + hop - 1
        return pltpu.make_async_remote_copy(
            src_ref=src if j == 0 else bank.at[mine],
            dst_ref=bank.at[origin if arriving else mine],
            send_sem=send.at[at],
            recv_sem=recv.at[at],
            device_id={"member": to},
            device_id_type=pl.DeviceIdType.MESH,
        )

    hops = sorted(range(1, outer), key=lambda j: (min(j, outer - j), j))

    def over_inner(do):
        def step(hop, c):
            do(hop)
            return c

        lax.fori_loop(1, inner, step, 0)

    def gather_start(src, bank, send, recv):
        over_inner(lambda hop: inner_copy(src, bank, 0, hop, send, recv).start())
        for j in hops:
            outer_copy(src, bank, j, send, recv).start()

    def forward(src, bank, j, send, recv):
        outer_copy(src, bank, j, send, recv, True).wait_recv()
        over_inner(lambda hop: inner_copy(src, bank, j, hop, send, recv).start())

    def gather_inner(src, bank, j, send, recv, use):
        def do(hop):
            inner_copy(src, bank, j, hop, send, recv, True).wait_recv()
            from_outer = lax.rem(me_outer + outer - j, outer)
            use(from_outer * inner + lax.rem(me_inner + inner - hop, inner))

        over_inner(do)

    def outer_origin(j):
        return lax.rem(me_outer + outer - j, outer) * inner + me_inner

    def gather_drain(src, bank, send, recv):
        for j in hops:
            outer_copy(src, bank, j, send, recv).wait_send()
        for j in range(outer):
            over_inner(lambda hop: inner_copy(src, bank, j, hop, send, recv).wait_send())

    def group_copy(bank, got, k, send, recv):
        to = lax.rem(g + k, groups)
        return pltpu.make_async_remote_copy(
            src_ref=bank.at[to],
            dst_ref=got.at[k],
            send_sem=send.at[k],
            recv_sem=recv.at[k],
            device_id={"group": to},
            device_id_type=pl.DeviceIdType.MESH,
        )

    for i in range(pieces):
        tile_copy(i).start()

    barrier = pltpu.get_barrier_semaphore()

    def greet_member(k, c):
        pl.semaphore_signal(
            barrier,
            inc=1,
            device_id={"member": lax.rem(me + k, n)},
            device_id_type=pl.DeviceIdType.MESH,
        )
        return c

    lax.fori_loop(1, n, greet_member, 0)
    for k in range(1, groups):
        pl.semaphore_signal(
            barrier,
            inc=1,
            device_id={"group": lax.rem(g + k, groups)},
            device_id_type=pl.DeviceIdType.MESH,
        )
    pl.semaphore_wait(barrier, n - 1 + groups - 1)

    ag1 = (feat_ref, gather1)
    sem1 = (ag1_send, ag1_recv)
    gather_start(*ag1, *sem1)

    for e in range(groups):
        shape = (cap * blocks, feat_ref.shape[1])
        line = lax.broadcasted_iota(jnp.int32, shape, 0)
        value = jnp.zeros(shape, F32)
        for c in range(cap):
            target = jnp.where(c < count_ref[0, e], c * blocks + mirror_ref[0, e, c], -1)
            value = jnp.where(line == target, 1.0, value)
        hot_ref[e] = value
    for k in range(1, groups):
        group_copy(hot_ref, got_hot, k, hot_send, hot_recv).start()

    slot = slot_ref[...]
    dest = slot // cap
    live = jnp.zeros(slot.shape, jnp.int32)
    for e in range(groups):
        live = jnp.where(dest == e, count_ref[0, e], live)
    key = jnp.where(slot - dest * cap < live, slot * columns + column_ref[...], -1)
    key_down = jnp.transpose(jnp.broadcast_to(key, (8, total)))[:, 0:1]
    earlier = lax.broadcasted_iota(jnp.int32, (total, total), 0)
    order = lax.broadcasted_iota(jnp.int32, (total, total), 1)
    same = (key_down == key) & (earlier < order)
    found = jnp.max(jnp.where(same, earlier, -1), axis=0, keepdims=True)
    prev_vmem[...] = jnp.where(found < 0, total, found)
    for i in range(0, slots * columns, total):
        found = jnp.max(
            jnp.where(key_down == order + i, earlier, -1), axis=0, keepdims=True
        )
        last_vmem[:, i : i + total] = jnp.where(found < 0, total, found)
    prev_copy = pltpu.make_async_copy(prev_vmem, prev_ref, table_sem.at[0])
    last_copy = pltpu.make_async_copy(last_vmem, last_ref, table_sem.at[1])
    prev_copy.start()
    last_copy.start()
    tile_buf[total] = jnp.zeros((size, size), BF16)
    run_buf[total] = jnp.zeros((size, size), F32)

    prev_copy.wait()
    last_copy.wait()

    def chain(t, c):
        value = tile_buf[t].astype(F32) + run_buf[prev_ref[0, t]]
        run_buf[t] = value
        tile_buf[t] = value.astype(BF16)
        return c

    for i in range(pieces):
        tile_copy(i).wait()
        lax.fori_loop(i * piece, (i + 1) * piece, chain, 0, unroll=4)
        if i % 2 == 1 and i // 2 < len(hops):
            forward(*ag1, hops[i // 2], *sem1)
    for j in hops[pieces // 2 :]:
        forward(*ag1, j, *sem1)

    def stage(origin, at):
        for s in range(slots):
            for b in range(blocks):
                stage_buf[at, s * size : (s + 1) * size, b * size : (b + 1) * size] = tile_buf[
                    last_ref[0, s * columns + origin * blocks + b]
                ]

    if keep:

        def stage_all(k, c):
            stage(k, k)
            return c

        lax.fori_loop(0, n, stage_all, 0)

    def place(origin):
        if keep:
            return origin
        stage(origin, 0)
        return 0

    def combine(part, got):
        sums = []
        for b in range(blocks):
            value = None
            for k in range(groups):
                hot = hot_ref[g] if k == 0 else got_hot[k]
                for c in range(cap):
                    block = (
                        part[g, c * size : (c + 1) * size, :]
                        if k == 0
                        else got[k, c * size : (c + 1) * size, :]
                    )
                    weight = hot[c * blocks + b : c * blocks + b + 1, :]
                    repeat = block.shape[1] // weight.shape[1]
                    if repeat > 1:
                        weight = jnp.concatenate([weight] * repeat, axis=1)
                    term = weight * block.astype(F32)
                    value = term if value is None else value + term
            sums.append(value.astype(BF16))
        return sums

    acc1[...] = jnp.dot(stage_buf[place(me)], feat_ref[...], preferred_element_type=F32)

    def first_layer(origin):
        at = place(origin)
        acc1[...] += jnp.dot(stage_buf[at], gather1[origin], preferred_element_type=F32)

    for j in hops:
        first_layer(outer_origin(j))
    for j in [0] + hops:
        gather_inner(*ag1, j, *sem1, first_layer)
    for e in range(groups):
        part1[e] = acc1[e * cap * size : (e + 1) * cap * size, :].astype(BF16)
    for k in range(1, groups):
        group_copy(part1, got1, k, rs1_send, rs1_recv).start()
    for k in range(1, groups):
        group_copy(hot_ref, got_hot, k, hot_send, hot_recv).wait_recv()
    for k in range(1, groups):
        group_copy(part1, got1, k, rs1_send, rs1_recv).wait_recv()
    sums = combine(part1, got1)
    for b in range(blocks):
        own_sum[b * size : (b + 1) * size, :] = sums[b]

    ag2 = (own_sum, gather2)
    sem2 = (ag2_send, ag2_recv)
    gather_start(*ag2, *sem2)

    def hidden_of(value):
        raw = jnp.dot(value, w1_ref[...], preferred_element_type=F32) + b1_ref[...]
        return jnp.maximum(raw, 0.0).astype(BF16)

    acc2[...] = jnp.dot(stage_buf[place(me)], hidden_of(own_sum[...]), preferred_element_type=F32)

    def second_layer(origin):
        at = place(origin)
        acc2[...] += jnp.dot(
            stage_buf[at], hidden_of(gather2[origin]), preferred_element_type=F32
        )

    waiting = []
    for j in hops:
        forward(*ag2, j, *sem2)
        for i in waiting:
            second_layer(outer_origin(i))
        waiting = [j]
        if j == hops[1]:
            gather_inner(*ag2, 0, *sem2, second_layer)
    for i in waiting:
        second_layer(outer_origin(i))
    for j in hops:
        gather_inner(*ag2, j, *sem2, second_layer)
    for e in range(groups):
        part2[e] = acc2[e * cap * size : (e + 1) * cap * size, :].astype(BF16)
    for k in range(1, groups):
        group_copy(part2, got2, k, rs2_send, rs2_recv).start()

    gather_drain(*ag1, *sem1)
    gather_drain(*ag2, *sem2)
    for k in range(1, groups):
        group_copy(hot_ref, got_hot, k, hot_send, hot_recv).wait_send()
        group_copy(part1, got1, k, rs1_send, rs1_recv).wait_send()
    for k in range(1, groups):
        group_copy(part2, got2, k, rs2_send, rs2_recv).wait_recv()
    sums = combine(part2, got2)
    for b in range(blocks):
        raw = jnp.dot(sums[b], w2_ref[...], preferred_element_type=F32) + b2_ref[...]
        out_ref[b * size : (b + 1) * size, :] = raw.astype(BF16)
    for k in range(1, groups):
        group_copy(part2, got2, k, rs2_send, rs2_recv).wait_send()


def general_body(
    features,
    edge_tiles,
    tile_slot,
    tile_column,
    mirror_count,
    mirror_block,
    weight_first,
    bias_first,
    weight_second,
    bias_second,
):
    groups = lax.axis_size("group")
    n = lax.axis_size("member")
    total, size, _ = edge_tiles.shape
    rows, width = features.shape
    hidden = weight_first.shape[1]
    outs = weight_second.shape[1]
    blocks = rows // size
    cap = mirror_block.shape[2]
    slots = groups * cap
    columns = n * blocks
    keep = slots * columns <= 2 * total
    pieces = 8 if total % 8 == 0 else 1
    outer = 4
    inner = n // outer
    vmem = pl.BlockSpec(memory_space=pltpu.VMEM)
    smem = pl.BlockSpec(memory_space=pltpu.SMEM)
    dma = pltpu.SemaphoreType.DMA
    return pl.pallas_call(
        functools.partial(general_kernel, outer, inner, groups, cap, keep),
        out_shape=jax.ShapeDtypeStruct((rows, outs), BF16),
        in_specs=[vmem, vmem, smem, smem, vmem, pl.BlockSpec(memory_space=pl.ANY)] + [vmem] * 4,
        out_specs=vmem,
        scratch_shapes=[
            pltpu.VMEM((total + 1, size, size), BF16),
            pltpu.VMEM((total + 1, size, size), F32),
            pltpu.VMEM((n if keep else 1, slots * size, rows), BF16),
            pltpu.VMEM((n, rows, width), BF16),
            pltpu.VMEM((n, rows, width), BF16),
            pltpu.VMEM((slots * size, width), F32),
            pltpu.VMEM((slots * size, hidden), F32),
            pltpu.VMEM((groups, cap * size, width), BF16),
            pltpu.VMEM((groups, cap * size, hidden), BF16),
            pltpu.VMEM((groups, cap * size, width), BF16),
            pltpu.VMEM((groups, cap * size, hidden), BF16),
            pltpu.VMEM((groups, cap * blocks, width), F32),
            pltpu.VMEM((rows, width), BF16),
            pltpu.VMEM((groups, cap * blocks, width), F32),
            pltpu.VMEM((1, total), jnp.int32),
            pltpu.VMEM((1, slots * columns), jnp.int32),
            pltpu.SMEM((1, total), jnp.int32),
            pltpu.SMEM((1, slots * columns), jnp.int32),
            dma((2,)),
            dma((pieces,)),
            dma((groups,)),
            dma((groups,)),
            dma((n,)),
            dma((n,)),
            dma((groups,)),
            dma((groups,)),
            dma((n,)),
            dma((n,)),
            dma((groups,)),
            dma((groups,)),
        ],
        compiler_params=pltpu.CompilerParams(
            collective_id=0, has_side_effects=True, vmem_limit_bytes=56 * 1024 * 1024
        ),
    )(
        tile_slot,
        tile_column,
        mirror_count,
        mirror_block,
        features,
        edge_tiles,
        weight_first,
        bias_first.reshape(1, -1),
        weight_second,
        bias_second.reshape(1, -1),
    )


def fast_kernel(
    slot_ref,
    column_ref,
    count_ref,
    mirror_ref,
    feat_ref,
    tiles_ref,
    w1_ref,
    b1_ref,
    w2_ref,
    b2_ref,
    out_ref,
    tile_buf,
    run_buf,
    stage_buf,
    bank1,
    bank2,
    acc1,
    acc2,
    part1,
    part2,
    got1,
    got2,
    got_hot,
    hot_ref,
    w1_top,
    w1_low,
    prev_vmem,
    last_vmem,
    prev_ref,
    last_ref,
    table_sem,
    tile_sem,
    hot_send,
    hot_recv,
    z_send,
    z_recv,
    x_send,
    x_recv,
    f_send,
    rs1_send,
    rs1_recv,
    rs2_send,
    rs2_recv,
):
    groups, cap, n = 4, 2, 8
    m = lax.axis_index("member")
    g = lax.axis_index("group")
    z, x = m // 2, lax.rem(m, 2)
    total, size = tiles_ref.shape[0], tiles_ref.shape[1]
    rows, width = feat_ref.shape
    blocks = rows // size
    slots = groups * cap
    columns = n * blocks
    pieces = tile_sem.shape[0]
    piece = total // pieces
    wing, fold = width // 2, rows // 2
    half = size // 2

    low = 1 - z // 2
    near = z + 1 - 2 * lax.rem(z, 2)
    line = [near, 1 + low, 3 * low]
    mid = lax.rem(z, 3) > 0
    partner = [g, g + 1 - 2 * lax.rem(g, 2), lax.rem(g + 2, groups), groups - 1 - g]

    def line_at(k):
        hi, lo = k // 2, lax.rem(k, 2)
        return (1 - hi) * ((1 - lo) * z + lo * line[0]) + hi * ((1 - lo) * line[1] + lo * line[2])

    def tile_copy(i):
        span = pl.ds(i * piece, piece)
        return pltpu.make_async_copy(tiles_ref.at[span], tile_buf.at[span], tile_sem.at[i])

    def to_member(bank, i, h, at, send, recv, device):
        block = bank.at[h, at]
        return pltpu.make_async_remote_copy(
            src_ref=block,
            dst_ref=block,
            send_sem=send,
            recv_sem=recv,
            device_id={"member": device},
            device_id_type=pl.DeviceIdType.MESH,
        )

    def z_copy(bank, i, h, to):
        return to_member(bank, i, h, m, z_send.at[i, h, to], z_recv.at[i, h, z], to * 2 + x)

    def z_arrival(bank, i, h, origin):
        return to_member(
            bank, i, h, origin * 2 + x, z_send.at[i, h, origin], z_recv.at[i, h, origin], origin * 2 + x
        )

    def far_copy(bank, i, h):
        return to_member(
            bank, i, h, line[2] * 2 + x, f_send.at[i, h], z_recv.at[i, h, line[2]], near * 2 + x
        )

    def x_copy(bank, i, h, origin):
        return to_member(
            bank, i, h, origin * 2 + x, x_send.at[i, h, origin], x_recv.at[i, h, origin], z * 2 + 1 - x
        )

    def x_arrival(bank, i, h, origin):
        return to_member(
            bank, i, h, origin * 2 + 1 - x, x_send.at[i, h, origin], x_recv.at[i, h, origin], z * 2 + 1 - x
        )

    def gather_start(bank, i, h):
        x_copy(bank, i, h, z).start()
        z_copy(bank, i, h, line[0]).start()
        z_copy(bank, i, h, line[1]).start()

        @pl.when(mid)
        def _():
            z_copy(bank, i, h, line[2]).start()

    def forward(bank, i, h, k):
        z_arrival(bank, i, h, line[k]).wait_recv()
        if k == 2:

            @pl.when(mid)
            def _():
                far_copy(bank, i, h).start()

        x_copy(bank, i, h, line[k]).start()

    def gather_drain(bank, i, h):
        z_copy(bank, i, h, line[0]).wait_send()
        z_copy(bank, i, h, line[1]).wait_send()

        @pl.when(mid)
        def _():
            z_copy(bank, i, h, line[2]).wait_send()
            far_copy(bank, i, h).wait_send()

        for k in range(4):
            x_copy(bank, i, h, (z, *line)[k]).wait_send()

    def group_copy(src, dst, j, send, recv):
        return pltpu.make_async_remote_copy(
            src_ref=src,
            dst_ref=dst,
            send_sem=send,
            recv_sem=recv,
            device_id={"group": partner[j]},
            device_id_type=pl.DeviceIdType.MESH,
        )

    def hot_copy(j):
        return group_copy(hot_ref.at[j], got_hot.at[j], j, hot_send.at[j], hot_recv.at[j])

    def rs1_copy(h, j):
        return group_copy(part1.at[h, j], got1.at[h, j], j, rs1_send.at[h, j], rs1_recv.at[h, j])

    def rs2_copy(r, j):
        return group_copy(part2.at[r, j], got2.at[r, j], j, rs2_send.at[r, j], rs2_recv.at[r, j])

    for i in range(pieces):
        tile_copy(i).start()

    barrier = pltpu.get_barrier_semaphore()

    def greet_member(k, c):
        pl.semaphore_signal(
            barrier,
            inc=1,
            device_id={"member": lax.rem(m + k, n)},
            device_id_type=pl.DeviceIdType.MESH,
        )
        return c

    lax.fori_loop(1, n, greet_member, 0)
    for j in range(1, groups):
        pl.semaphore_signal(
            barrier,
            inc=1,
            device_id={"group": partner[j]},
            device_id_type=pl.DeviceIdType.MESH,
        )

    def turn(value):
        return pltpu.roll(value.astype(F32), wing, 1)

    lane = lax.broadcasted_iota(jnp.int32, (fold, width), 1)
    left = lane < wing
    for h in range(2):
        top, bottom = feat_ref[0:fold, :].astype(F32), feat_ref[fold:rows, :].astype(F32)
        packed = jnp.where(left, top, turn(bottom)) if h == 0 else jnp.where(left, turn(top), bottom)
        bank1[h, m] = packed.astype(BF16)

    for j in range(groups):
        shape = (cap * blocks, width)
        row = lax.broadcasted_iota(jnp.int32, shape, 0)
        value = jnp.zeros(shape, F32)
        for c in range(cap):
            e = partner[j]
            target = jnp.where(c < count_ref[0, e], c * blocks + mirror_ref[0, c, e], -1)
            value = jnp.where(row == target, 1.0, value)
        hot_ref[j] = value

    pl.semaphore_wait(barrier, n - 1 + groups - 1)

    for h in range(2):
        gather_start(bank1, 0, h)
    for j in range(1, groups):
        hot_copy(j).start()

    slot = slot_ref[...]
    dest = slot // cap
    live = jnp.zeros(slot.shape, jnp.int32)
    for e in range(groups):
        live = jnp.where(dest == e, count_ref[0, e], live)
    key = jnp.where(slot - dest * cap < live, slot * columns + column_ref[...], -1)
    key_down = jnp.transpose(jnp.broadcast_to(key, (8, total)))[:, 0:1]
    earlier = lax.broadcasted_iota(jnp.int32, (total, total), 0)
    order = lax.broadcasted_iota(jnp.int32, (total, total), 1)
    same = (key_down == key) & (earlier < order)
    found = jnp.max(jnp.where(same, earlier, -1), axis=0, keepdims=True)
    prev_vmem[...] = jnp.where(found < 0, total, found)
    for i in range(0, slots * columns, total):
        found = jnp.max(jnp.where(key_down == order + i, earlier, -1), axis=0, keepdims=True)
        last_vmem[:, i : i + total] = jnp.where(found < 0, total, found)
    prev_copy = pltpu.make_async_copy(prev_vmem, prev_ref, table_sem.at[0])
    last_copy = pltpu.make_async_copy(last_vmem, last_ref, table_sem.at[1])
    prev_copy.start()
    last_copy.start()
    tile_buf[total] = jnp.zeros((size, size), BF16)
    run_buf[total] = jnp.zeros((size, size), F32)
    w1_top[...] = jnp.zeros(w1_top.shape, BF16)
    w1_low[...] = jnp.zeros(w1_low.shape, BF16)
    for h in range(2):
        w1_top[h * width : h * width + wing, :] = w1_ref[h * wing : (h + 1) * wing, :]
        w1_low[h * width + wing : (h + 1) * width, :] = w1_ref[h * wing : (h + 1) * wing, :]
    prev_copy.wait()
    last_copy.wait()

    def chain(t, c):
        value = tile_buf[t].astype(F32) + run_buf[prev_ref[0, t]]
        run_buf[t] = value
        tile_buf[t] = value.astype(BF16)
        return c

    for i in range(pieces):
        tile_copy(i).wait()
        lax.fori_loop(i * piece, (i + 1) * piece, chain, 0, unroll=4)
        if i in FORWARD_AT:
            forward(bank1, 0, *FORWARD_AT[i])

    def stage(k, c):
        for s in range(slots):
            for b in range(blocks):
                stage_buf[k, s * size : (s + 1) * size, b * size : (b + 1) * size] = tile_buf[
                    last_ref[0, s * columns + k * blocks + b]
                ]
        return c

    lax.fori_loop(0, n, stage, 0)

    def first_layer(h, origin, fresh):
        packed = bank1[h, origin]
        sources = jnp.concatenate([packed, turn(packed).astype(BF16)], axis=0)
        value = jnp.dot(stage_buf[origin], sources, preferred_element_type=F32)
        if fresh:
            acc1[h] = value
        else:
            acc1[h] += value

    def first_line(h):
        first_layer(h, m, True)

        def step(k, c):
            first_layer(h, line_at(k) * 2 + x, False)
            return c

        lax.fori_loop(1, 4, step, 0)

    def first_across(h, start, stop):
        def step(k, c):
            x_arrival(bank1, 0, h, line_at(k)).wait_recv()
            first_layer(h, line_at(k) * 2 + 1 - x, False)
            return c

        lax.fori_loop(start, stop, step, 0)

    def exchange_first(h):
        keep_left = lax.broadcasted_iota(jnp.int32, (size, width), 1) < wing
        for j in (2, 3, 1, 0):
            at = pl.multiple_of(partner[j] * cap * size, cap * size)
            one = acc1[h, pl.ds(at, size), :]
            two = acc1[h, pl.ds(at + size, size), :]
            part1[h, j] = jnp.where(keep_left, one, pltpu.roll(two, wing, 1)).astype(BF16)
            if j:
                rs1_copy(h, j).start()

    def sum_first(h):
        keep_left = lax.broadcasted_iota(jnp.int32, (size, width), 1) < wing
        row_left = lax.broadcasted_iota(jnp.int32, (1, width), 1) < wing
        for j in range(1, groups):
            rs1_copy(h, j).wait_recv()
        sums = []
        for b in range(blocks):
            value = None
            for j in range(groups):
                hot = hot_ref[0] if j == 0 else got_hot[j]
                weight = jnp.where(row_left, hot[b : b + 1, :], hot[blocks + b : blocks + b + 1, :])
                block = part1[h, 0] if j == 0 else got1[h, j]
                term = weight * block.astype(F32)
                value = term if value is None else value + term
            sums.append(value + pltpu.roll(value, wing, 1))
        for b in range(blocks // 2):
            bank2[h, m, b * size : (b + 1) * size, :] = jnp.where(
                keep_left, sums[b], sums[b + blocks // 2]
            ).astype(BF16)

    forward(bank1, 0, 1, 0)
    first_line(0)
    first_across(0, 0, 2)
    forward(bank1, 0, 1, 1)
    first_across(0, 2, 3)
    forward(bank1, 0, 1, 2)
    first_across(0, 3, 4)
    exchange_first(0)
    first_line(1)
    for j in range(1, groups):
        hot_copy(j).wait_recv()
    sum_first(0)
    gather_start(bank2, 1, 0)
    first_across(1, 0, 4)
    exchange_first(1)
    forward(bank2, 1, 0, 0)
    forward(bank2, 1, 0, 1)
    sum_first(1)
    gather_start(bank2, 1, 1)
    forward(bank2, 1, 0, 2)

    def hidden_of(origin):
        packed = jnp.concatenate([bank2[0, origin], bank2[1, origin]], axis=1)
        parts = []
        for w in (w1_top, w1_low):
            raw = jnp.dot(packed, w[...], preferred_element_type=F32) + b1_ref[...]
            parts.append(jnp.maximum(raw, 0.0).astype(BF16))
        return jnp.concatenate(parts, axis=0)

    def second_layer(origin):
        acc2[...] += jnp.dot(stage_buf[origin], hidden_of(origin), preferred_element_type=F32)

    acc2[...] = jnp.dot(stage_buf[m], hidden_of(m), preferred_element_type=F32)
    for k in range(3):
        forward(bank2, 1, 1, k)

    def second_line(k, c):
        second_layer(line_at(k) * 2 + x)
        return c

    lax.fori_loop(1, 4, second_line, 0)

    def second_across(k, c):
        for h in range(2):
            x_arrival(bank2, 1, h, line_at(k)).wait_recv()
        second_layer(line_at(k) * 2 + 1 - x)
        return c

    lax.fori_loop(0, 3, second_across, 0)
    for h in range(2):
        x_arrival(bank2, 1, h, line_at(3)).wait_recv()
    last = line_at(3) * 2 + 1 - x
    hidden = hidden_of(last)
    for j in (2, 3, 1, 0):
        at = pl.ds(pl.multiple_of(partner[j] * cap * size, cap * size), cap * size)
        value = acc2[at, :] + jnp.dot(stage_buf[last, at, :], hidden, preferred_element_type=F32)
        for r in range(2):
            for c in range(cap):
                part2[r, j, c * half : (c + 1) * half, :] = value[
                    c * size + r * half : c * size + (r + 1) * half, :
                ].astype(BF16)
        if j == 2:
            rs2_copy(0, 2).start()
        elif j == 3:
            rs2_copy(0, 3).start()
            rs2_copy(1, 2).start()
            rs2_copy(1, 3).start()
        elif j == 1:
            rs2_copy(0, 1).start()
            rs2_copy(1, 1).start()

    for i, bank in enumerate((bank1, bank2)):
        for h in range(2):
            gather_drain(bank, i, h)
    for j in range(1, groups):
        hot_copy(j).wait_send()
        for h in range(2):
            rs1_copy(h, j).wait_send()

    for r in range(2):
        for j in (1, 2, 3):
            rs2_copy(r, j).wait_recv()
        sums = []
        for b in range(blocks):
            value = None
            for j in range(groups):
                hot = hot_ref[0] if j == 0 else got_hot[j]
                for c in range(cap):
                    weight = hot[c * blocks + b : c * blocks + b + 1, :]
                    weight = jnp.concatenate([weight] * (w2_ref.shape[0] // width), axis=1)
                    span = slice(c * half, (c + 1) * half)
                    block = part2[r, 0, span, :] if j == 0 else got2[r, j, span, :]
                    term = weight * block.astype(F32)
                    value = term if value is None else value + term
            sums.append(value.astype(BF16))
        raw = jnp.dot(jnp.concatenate(sums, axis=0), w2_ref[...], preferred_element_type=F32)
        raw = (raw + b2_ref[...]).astype(BF16)
        for b in range(blocks):
            out_ref[b * size + r * half : b * size + (r + 1) * half, :] = raw[
                b * half : (b + 1) * half, :
            ]
    for r in range(2):
        for j in (1, 2, 3):
            rs2_copy(r, j).wait_send()


FORWARD_AT = {3: (0, 0), 5: (0, 1), 7: (0, 2)}


def fast_body(
    features,
    edge_tiles,
    tile_slot,
    tile_column,
    mirror_count,
    mirror_block,
    weight_first,
    bias_first,
    weight_second,
    bias_second,
):
    groups = lax.axis_size("group")
    n = lax.axis_size("member")
    total, size, _ = edge_tiles.shape
    rows, width = features.shape
    hidden = weight_first.shape[1]
    outs = weight_second.shape[1]
    blocks = rows // size
    cap = mirror_block.shape[2]
    slots = groups * cap
    columns = n * blocks
    pieces = 8
    fold = rows // 2
    vmem = pl.BlockSpec(memory_space=pltpu.VMEM)
    smem = pl.BlockSpec(memory_space=pltpu.SMEM)
    dma = pltpu.SemaphoreType.DMA
    return pl.pallas_call(
        fast_kernel,
        out_shape=jax.ShapeDtypeStruct((rows, outs), BF16),
        in_specs=[vmem, vmem, smem, smem, vmem, pl.BlockSpec(memory_space=pl.ANY)] + [vmem] * 4,
        out_specs=vmem,
        scratch_shapes=[
            pltpu.VMEM((total + 1, size, size), BF16),
            pltpu.VMEM((total + 1, size, size), F32),
            pltpu.VMEM((n, slots * size, rows), BF16),
            pltpu.VMEM((2, n, fold, width), BF16),
            pltpu.VMEM((2, n, fold, width), BF16),
            pltpu.VMEM((2, slots * size, width), F32),
            pltpu.VMEM((slots * size, hidden), F32),
            pltpu.VMEM((2, groups, size, width), BF16),
            pltpu.VMEM((2, groups, size, hidden), BF16),
            pltpu.VMEM((2, groups, size, width), BF16),
            pltpu.VMEM((2, groups, size, hidden), BF16),
            pltpu.VMEM((groups, cap * blocks, width), F32),
            pltpu.VMEM((groups, cap * blocks, width), F32),
            pltpu.VMEM((2 * width, hidden), BF16),
            pltpu.VMEM((2 * width, hidden), BF16),
            pltpu.VMEM((1, total), jnp.int32),
            pltpu.VMEM((1, slots * columns), jnp.int32),
            pltpu.SMEM((1, total), jnp.int32),
            pltpu.SMEM((1, slots * columns), jnp.int32),
            dma((2,)),
            dma((pieces,)),
            dma((groups,)),
            dma((groups,)),
            dma((2, 2, 4)),
            dma((2, 2, 4)),
            dma((2, 2, 4)),
            dma((2, 2, 4)),
            dma((2, 2)),
            dma((2, groups)),
            dma((2, groups)),
            dma((2, groups)),
            dma((2, groups)),
        ],
        compiler_params=pltpu.CompilerParams(
            collective_id=1, has_side_effects=True, vmem_limit_bytes=56 * 1024 * 1024
        ),
    )(
        tile_slot,
        tile_column,
        mirror_count,
        jnp.transpose(mirror_block, (0, 2, 1)),
        features,
        edge_tiles,
        weight_first,
        bias_first.reshape(1, -1),
        weight_second,
        bias_second.reshape(1, -1),
    )


def body(features, edge_tiles, tile_slot, tile_column, mirror_count, mirror_block, *weights):
    small = lax.axis_size("member") == 8 and lax.axis_size("group") == 4
    args = (features, edge_tiles, tile_slot, tile_column, mirror_count, mirror_block, *weights)
    return fast_body(*args) if small else general_body(*args)


def solution(mesh):
    placed = (
        P(("group", "member"), None),
        P(("group", "member"), None, None),
        P(("group", "member"), None),
        P(("group", "member"), None),
        P(("group", "member"), None),
        P(("group", "member"), None, None),
        P(),
        P(),
        P(),
        P(),
    )
    return jax.shard_map(
        body, mesh=mesh, in_specs=placed, out_specs=P(("group", "member"), None), check_vma=False
    )
```

```python
import functools

import jax
import jax.numpy as jnp
from jax import lax
from jax.experimental import pallas as pl
from jax.experimental.pallas import tpu as pltpu
from jax.sharding import PartitionSpec as P

F32 = jnp.float32
BF16 = jnp.bfloat16


def general_kernel(
    outer,
    inner,
    groups,
    cap,
    keep,
    slot_ref,
    column_ref,
    count_ref,
    mirror_ref,
    feat_ref,
    tiles_ref,
    w1_ref,
    b1_ref,
    w2_ref,
    b2_ref,
    out_ref,
    tile_buf,
    run_buf,
    stage_buf,
    gather1,
    gather2,
    acc1,
    acc2,
    part1,
    part2,
    got1,
    got2,
    got_hot,
    own_sum,
    hot_ref,
    prev_vmem,
    last_vmem,
    prev_ref,
    last_ref,
    table_sem,
    tile_sem,
    hot_send,
    hot_recv,
    ag1_send,
    ag1_recv,
    rs1_send,
    rs1_recv,
    ag2_send,
    ag2_recv,
    rs2_send,
    rs2_recv,
):
    n = outer * inner
    me = lax.axis_index("member")
    me_outer, me_inner = me // inner, lax.rem(me, inner)
    g = lax.axis_index("group")
    total = tiles_ref.shape[0]
    size = tiles_ref.shape[1]
    rows = feat_ref.shape[0]
    blocks = rows // size
    slots = groups * cap
    columns = n * blocks
    pieces = tile_sem.shape[0]
    piece = total // pieces

    def tile_copy(i):
        span = pl.ds(i * piece, piece)
        return pltpu.make_async_copy(tiles_ref.at[span], tile_buf.at[span], tile_sem.at[i])

    def outer_copy(src, bank, j, send, recv, arriving=False):
        from_outer = lax.rem(me_outer + outer - j, outer)
        origin = from_outer * inner + me_inner
        to = lax.rem(me_outer + j, outer) * inner + me_inner
        return pltpu.make_async_remote_copy(
            src_ref=src,
            dst_ref=bank.at[origin if arriving else me],
            send_sem=send.at[j],
            recv_sem=recv.at[j],
            device_id={"member": to},
            device_id_type=pl.DeviceIdType.MESH,
        )

    def inner_copy(src, bank, j, hop, send, recv, arriving=False):
        from_outer = lax.rem(me_outer + outer - j, outer)
        from_inner = lax.rem(me_inner + inner - hop, inner)
        mine = from_outer * inner + me_inner
        origin = from_outer * inner + from_inner
        to = me_outer * inner + lax.rem(me_inner + hop, inner)
        at = outer + j * (inner - 1) + hop - 1
        return pltpu.make_async_remote_copy(
            src_ref=src if j == 0 else bank.at[mine],
            dst_ref=bank.at[origin if arriving else mine],
            send_sem=send.at[at],
            recv_sem=recv.at[at],
            device_id={"member": to},
            device_id_type=pl.DeviceIdType.MESH,
        )

    hops = sorted(range(1, outer), key=lambda j: (min(j, outer - j), j))

    def over_inner(do):
        def step(hop, c):
            do(hop)
            return c

        lax.fori_loop(1, inner, step, 0)

    def gather_start(src, bank, send, recv):
        over_inner(lambda hop: inner_copy(src, bank, 0, hop, send, recv).start())
        for j in hops:
            outer_copy(src, bank, j, send, recv).start()

    def forward(src, bank, j, send, recv):
        outer_copy(src, bank, j, send, recv, True).wait_recv()
        over_inner(lambda hop: inner_copy(src, bank, j, hop, send, recv).start())

    def gather_inner(src, bank, j, send, recv, use):
        def do(hop):
            inner_copy(src, bank, j, hop, send, recv, True).wait_recv()
            from_outer = lax.rem(me_outer + outer - j, outer)
            use(from_outer * inner + lax.rem(me_inner + inner - hop, inner))

        over_inner(do)

    def outer_origin(j):
        return lax.rem(me_outer + outer - j, outer) * inner + me_inner

    def gather_drain(src, bank, send, recv):
        for j in hops:
            outer_copy(src, bank, j, send, recv).wait_send()
        for j in range(outer):
            over_inner(lambda hop: inner_copy(src, bank, j, hop, send, recv).wait_send())

    def group_copy(bank, got, k, send, recv):
        to = lax.rem(g + k, groups)
        return pltpu.make_async_remote_copy(
            src_ref=bank.at[to],
            dst_ref=got.at[k],
            send_sem=send.at[k],
            recv_sem=recv.at[k],
            device_id={"group": to},
            device_id_type=pl.DeviceIdType.MESH,
        )

    for i in range(pieces):
        tile_copy(i).start()

    barrier = pltpu.get_barrier_semaphore()

    def greet_member(k, c):
        pl.semaphore_signal(
            barrier,
            inc=1,
            device_id={"member": lax.rem(me + k, n)},
            device_id_type=pl.DeviceIdType.MESH,
        )
        return c

    lax.fori_loop(1, n, greet_member, 0)
    for k in range(1, groups):
        pl.semaphore_signal(
            barrier,
            inc=1,
            device_id={"group": lax.rem(g + k, groups)},
            device_id_type=pl.DeviceIdType.MESH,
        )
    pl.semaphore_wait(barrier, n - 1 + groups - 1)

    ag1 = (feat_ref, gather1)
    sem1 = (ag1_send, ag1_recv)
    gather_start(*ag1, *sem1)

    for e in range(groups):
        shape = (cap * blocks, feat_ref.shape[1])
        line = lax.broadcasted_iota(jnp.int32, shape, 0)
        value = jnp.zeros(shape, F32)
        for c in range(cap):
            target = jnp.where(c < count_ref[0, e], c * blocks + mirror_ref[0, e, c], -1)
            value = jnp.where(line == target, 1.0, value)
        hot_ref[e] = value
    for k in range(1, groups):
        group_copy(hot_ref, got_hot, k, hot_send, hot_recv).start()

    slot = slot_ref[...]
    dest = slot // cap
    live = jnp.zeros(slot.shape, jnp.int32)
    for e in range(groups):
        live = jnp.where(dest == e, count_ref[0, e], live)
    key = jnp.where(slot - dest * cap < live, slot * columns + column_ref[...], -1)
    key_down = jnp.transpose(jnp.broadcast_to(key, (8, total)))[:, 0:1]
    earlier = lax.broadcasted_iota(jnp.int32, (total, total), 0)
    order = lax.broadcasted_iota(jnp.int32, (total, total), 1)
    same = (key_down == key) & (earlier < order)
    found = jnp.max(jnp.where(same, earlier, -1), axis=0, keepdims=True)
    prev_vmem[...] = jnp.where(found < 0, total, found)
    for i in range(0, slots * columns, total):
        found = jnp.max(
            jnp.where(key_down == order + i, earlier, -1), axis=0, keepdims=True
        )
        last_vmem[:, i : i + total] = jnp.where(found < 0, total, found)
    prev_copy = pltpu.make_async_copy(prev_vmem, prev_ref, table_sem.at[0])
    last_copy = pltpu.make_async_copy(last_vmem, last_ref, table_sem.at[1])
    prev_copy.start()
    last_copy.start()
    tile_buf[total] = jnp.zeros((size, size), BF16)
    run_buf[total] = jnp.zeros((size, size), F32)

    prev_copy.wait()
    last_copy.wait()

    def chain(t, c):
        value = tile_buf[t].astype(F32) + run_buf[prev_ref[0, t]]
        run_buf[t] = value
        tile_buf[t] = value.astype(BF16)
        return c

    for i in range(pieces):
        tile_copy(i).wait()
        lax.fori_loop(i * piece, (i + 1) * piece, chain, 0, unroll=4)
        if i % 2 == 1 and i // 2 < len(hops):
            forward(*ag1, hops[i // 2], *sem1)
    for j in hops[pieces // 2 :]:
        forward(*ag1, j, *sem1)

    def stage(origin, at):
        for s in range(slots):
            for b in range(blocks):
                stage_buf[at, s * size : (s + 1) * size, b * size : (b + 1) * size] = tile_buf[
                    last_ref[0, s * columns + origin * blocks + b]
                ]

    if keep:

        def stage_all(k, c):
            stage(k, k)
            return c

        lax.fori_loop(0, n, stage_all, 0)

    def place(origin):
        if keep:
            return origin
        stage(origin, 0)
        return 0

    def combine(part, got):
        sums = []
        for b in range(blocks):
            value = None
            for k in range(groups):
                hot = hot_ref[g] if k == 0 else got_hot[k]
                for c in range(cap):
                    block = (
                        part[g, c * size : (c + 1) * size, :]
                        if k == 0
                        else got[k, c * size : (c + 1) * size, :]
                    )
                    weight = hot[c * blocks + b : c * blocks + b + 1, :]
                    repeat = block.shape[1] // weight.shape[1]
                    if repeat > 1:
                        weight = jnp.concatenate([weight] * repeat, axis=1)
                    term = weight * block.astype(F32)
                    value = term if value is None else value + term
            sums.append(value.astype(BF16))
        return sums

    acc1[...] = jnp.dot(stage_buf[place(me)], feat_ref[...], preferred_element_type=F32)

    def first_layer(origin):
        at = place(origin)
        acc1[...] += jnp.dot(stage_buf[at], gather1[origin], preferred_element_type=F32)

    for j in hops:
        first_layer(outer_origin(j))
    for j in [0] + hops:
        gather_inner(*ag1, j, *sem1, first_layer)
    for e in range(groups):
        part1[e] = acc1[e * cap * size : (e + 1) * cap * size, :].astype(BF16)
    for k in range(1, groups):
        group_copy(part1, got1, k, rs1_send, rs1_recv).start()
    for k in range(1, groups):
        group_copy(hot_ref, got_hot, k, hot_send, hot_recv).wait_recv()
    for k in range(1, groups):
        group_copy(part1, got1, k, rs1_send, rs1_recv).wait_recv()
    sums = combine(part1, got1)
    for b in range(blocks):
        own_sum[b * size : (b + 1) * size, :] = sums[b]

    ag2 = (own_sum, gather2)
    sem2 = (ag2_send, ag2_recv)
    gather_start(*ag2, *sem2)

    def hidden_of(value):
        raw = jnp.dot(value, w1_ref[...], preferred_element_type=F32) + b1_ref[...]
        return jnp.maximum(raw, 0.0).astype(BF16)

    acc2[...] = jnp.dot(stage_buf[place(me)], hidden_of(own_sum[...]), preferred_element_type=F32)

    def second_layer(origin):
        at = place(origin)
        acc2[...] += jnp.dot(
            stage_buf[at], hidden_of(gather2[origin]), preferred_element_type=F32
        )

    waiting = []
    for j in hops:
        forward(*ag2, j, *sem2)
        for i in waiting:
            second_layer(outer_origin(i))
        waiting = [j]
        if j == hops[1]:
            gather_inner(*ag2, 0, *sem2, second_layer)
    for i in waiting:
        second_layer(outer_origin(i))
    for j in hops:
        gather_inner(*ag2, j, *sem2, second_layer)
    for e in range(groups):
        part2[e] = acc2[e * cap * size : (e + 1) * cap * size, :].astype(BF16)
    for k in range(1, groups):
        group_copy(part2, got2, k, rs2_send, rs2_recv).start()

    gather_drain(*ag1, *sem1)
    gather_drain(*ag2, *sem2)
    for k in range(1, groups):
        group_copy(hot_ref, got_hot, k, hot_send, hot_recv).wait_send()
        group_copy(part1, got1, k, rs1_send, rs1_recv).wait_send()
    for k in range(1, groups):
        group_copy(part2, got2, k, rs2_send, rs2_recv).wait_recv()
    sums = combine(part2, got2)
    for b in range(blocks):
        raw = jnp.dot(sums[b], w2_ref[...], preferred_element_type=F32) + b2_ref[...]
        out_ref[b * size : (b + 1) * size, :] = raw.astype(BF16)
    for k in range(1, groups):
        group_copy(part2, got2, k, rs2_send, rs2_recv).wait_send()


def general_body(
    features,
    edge_tiles,
    tile_slot,
    tile_column,
    mirror_count,
    mirror_block,
    weight_first,
    bias_first,
    weight_second,
    bias_second,
):
    groups = lax.axis_size("group")
    n = lax.axis_size("member")
    total, size, _ = edge_tiles.shape
    rows, width = features.shape
    hidden = weight_first.shape[1]
    outs = weight_second.shape[1]
    blocks = rows // size
    cap = mirror_block.shape[2]
    slots = groups * cap
    columns = n * blocks
    keep = slots * columns <= 2 * total
    pieces = 8 if total % 8 == 0 else 1
    outer = 4
    inner = n // outer
    vmem = pl.BlockSpec(memory_space=pltpu.VMEM)
    smem = pl.BlockSpec(memory_space=pltpu.SMEM)
    dma = pltpu.SemaphoreType.DMA
    return pl.pallas_call(
        functools.partial(general_kernel, outer, inner, groups, cap, keep),
        out_shape=jax.ShapeDtypeStruct((rows, outs), BF16),
        in_specs=[vmem, vmem, smem, smem, vmem, pl.BlockSpec(memory_space=pl.ANY)] + [vmem] * 4,
        out_specs=vmem,
        scratch_shapes=[
            pltpu.VMEM((total + 1, size, size), BF16),
            pltpu.VMEM((total + 1, size, size), F32),
            pltpu.VMEM((n if keep else 1, slots * size, rows), BF16),
            pltpu.VMEM((n, rows, width), BF16),
            pltpu.VMEM((n, rows, width), BF16),
            pltpu.VMEM((slots * size, width), F32),
            pltpu.VMEM((slots * size, hidden), F32),
            pltpu.VMEM((groups, cap * size, width), BF16),
            pltpu.VMEM((groups, cap * size, hidden), BF16),
            pltpu.VMEM((groups, cap * size, width), BF16),
            pltpu.VMEM((groups, cap * size, hidden), BF16),
            pltpu.VMEM((groups, cap * blocks, width), F32),
            pltpu.VMEM((rows, width), BF16),
            pltpu.VMEM((groups, cap * blocks, width), F32),
            pltpu.VMEM((1, total), jnp.int32),
            pltpu.VMEM((1, slots * columns), jnp.int32),
            pltpu.SMEM((1, total), jnp.int32),
            pltpu.SMEM((1, slots * columns), jnp.int32),
            dma((2,)),
            dma((pieces,)),
            dma((groups,)),
            dma((groups,)),
            dma((n,)),
            dma((n,)),
            dma((groups,)),
            dma((groups,)),
            dma((n,)),
            dma((n,)),
            dma((groups,)),
            dma((groups,)),
        ],
        compiler_params=pltpu.CompilerParams(
            collective_id=0, has_side_effects=True, vmem_limit_bytes=56 * 1024 * 1024
        ),
    )(
        tile_slot,
        tile_column,
        mirror_count,
        mirror_block,
        features,
        edge_tiles,
        weight_first,
        bias_first.reshape(1, -1),
        weight_second,
        bias_second.reshape(1, -1),
    )


def fast_kernel(
    slot_ref,
    column_ref,
    count_ref,
    mirror_ref,
    feat_ref,
    tiles_ref,
    w1_ref,
    b1_ref,
    w2_ref,
    b2_ref,
    out_ref,
    tile_buf,
    run_buf,
    stage_buf,
    bank1,
    bank2,
    acc1,
    acc2,
    part1,
    part2,
    got1,
    got2,
    got_hot,
    hot_ref,
    w1_top,
    w1_low,
    prev_vmem,
    last_vmem,
    prev_ref,
    last_ref,
    table_sem,
    tile_sem,
    hot_send,
    hot_recv,
    z_send,
    z_recv,
    x_send,
    x_recv,
    f_send,
    rs1_send,
    rs1_recv,
    rs2_send,
    rs2_recv,
):
    groups, cap, n = 4, 2, 8
    m = lax.axis_index("member")
    g = lax.axis_index("group")
    z, x = m // 2, lax.rem(m, 2)
    total, size = tiles_ref.shape[0], tiles_ref.shape[1]
    rows, width = feat_ref.shape
    blocks = rows // size
    slots = groups * cap
    columns = n * blocks
    pieces = tile_sem.shape[0]
    piece = total // pieces
    wing, fold = width // 2, rows // 2
    half = size // 2

    low = 1 - z // 2
    near = z + 1 - 2 * lax.rem(z, 2)
    line = [near, 1 + low, 3 * low]
    mid = lax.rem(z, 3) > 0
    partner = [g, g + 1 - 2 * lax.rem(g, 2), lax.rem(g + 2, groups), groups - 1 - g]

    def line_at(k):
        hi, lo = k // 2, lax.rem(k, 2)
        return (1 - hi) * ((1 - lo) * z + lo * line[0]) + hi * ((1 - lo) * line[1] + lo * line[2])

    def tile_copy(i):
        span = pl.ds(i * piece, piece)
        return pltpu.make_async_copy(tiles_ref.at[span], tile_buf.at[span], tile_sem.at[i])

    def to_member(bank, i, h, at, send, recv, device):
        block = bank.at[h, at]
        return pltpu.make_async_remote_copy(
            src_ref=block,
            dst_ref=block,
            send_sem=send,
            recv_sem=recv,
            device_id={"member": device},
            device_id_type=pl.DeviceIdType.MESH,
        )

    def z_copy(bank, i, h, to):
        return to_member(bank, i, h, m, z_send.at[i, h, to], z_recv.at[i, h, z], to * 2 + x)

    def z_arrival(bank, i, h, origin):
        return to_member(
            bank, i, h, origin * 2 + x, z_send.at[i, h, origin], z_recv.at[i, h, origin], origin * 2 + x
        )

    def far_copy(bank, i, h):
        return to_member(
            bank, i, h, line[2] * 2 + x, f_send.at[i, h], z_recv.at[i, h, line[2]], near * 2 + x
        )

    def x_copy(bank, i, h, origin):
        return to_member(
            bank, i, h, origin * 2 + x, x_send.at[i, h, origin], x_recv.at[i, h, origin], z * 2 + 1 - x
        )

    def x_arrival(bank, i, h, origin):
        return to_member(
            bank, i, h, origin * 2 + 1 - x, x_send.at[i, h, origin], x_recv.at[i, h, origin], z * 2 + 1 - x
        )

    def gather_start(bank, i, h):
        x_copy(bank, i, h, z).start()
        z_copy(bank, i, h, line[0]).start()
        z_copy(bank, i, h, line[1]).start()
        z_copy(bank, i, h, line[2]).start()

    def forward(bank, i, h, k):
        z_arrival(bank, i, h, line[k]).wait_recv()
        x_copy(bank, i, h, line[k]).start()

    def gather_drain(bank, i, h):
        z_copy(bank, i, h, line[0]).wait_send()
        z_copy(bank, i, h, line[1]).wait_send()
        z_copy(bank, i, h, line[2]).wait_send()

        for k in range(4):
            x_copy(bank, i, h, (z, *line)[k]).wait_send()

    def group_copy(src, dst, j, send, recv):
        return pltpu.make_async_remote_copy(
            src_ref=src,
            dst_ref=dst,
            send_sem=send,
            recv_sem=recv,
            device_id={"group": partner[j]},
            device_id_type=pl.DeviceIdType.MESH,
        )

    def hot_copy(j):
        return group_copy(hot_ref.at[j], got_hot.at[j], j, hot_send.at[j], hot_recv.at[j])

    def rs1_copy(h, j):
        return group_copy(part1.at[h, j], got1.at[h, j], j, rs1_send.at[h, j], rs1_recv.at[h, j])

    def rs2_copy(r, j):
        return group_copy(part2.at[r, j], got2.at[r, j], j, rs2_send.at[r, j], rs2_recv.at[r, j])

    for i in range(pieces):
        tile_copy(i).start()

    barrier = pltpu.get_barrier_semaphore()

    def greet_member(k, c):
        pl.semaphore_signal(
            barrier,
            inc=1,
            device_id={"member": lax.rem(m + k, n)},
            device_id_type=pl.DeviceIdType.MESH,
        )
        return c

    lax.fori_loop(1, n, greet_member, 0)
    for j in range(1, groups):
        pl.semaphore_signal(
            barrier,
            inc=1,
            device_id={"group": partner[j]},
            device_id_type=pl.DeviceIdType.MESH,
        )

    def turn(value):
        return pltpu.roll(value.astype(F32), wing, 1)

    lane = lax.broadcasted_iota(jnp.int32, (fold, width), 1)
    left = lane < wing
    for h in range(2):
        top, bottom = feat_ref[0:fold, :].astype(F32), feat_ref[fold:rows, :].astype(F32)
        packed = jnp.where(left, top, turn(bottom)) if h == 0 else jnp.where(left, turn(top), bottom)
        bank1[h, m] = packed.astype(BF16)

    for j in range(groups):
        shape = (cap * blocks, width)
        row = lax.broadcasted_iota(jnp.int32, shape, 0)
        value = jnp.zeros(shape, F32)
        for c in range(cap):
            e = partner[j]
            target = jnp.where(c < count_ref[0, e], c * blocks + mirror_ref[0, c, e], -1)
            value = jnp.where(row == target, 1.0, value)
        hot_ref[j] = value

    pl.semaphore_wait(barrier, n - 1 + groups - 1)

    gather_start(bank1, 0, 0)
    for j in range(1, groups):
        hot_copy(j).start()

    slot = slot_ref[...]
    dest = slot // cap
    live = jnp.zeros(slot.shape, jnp.int32)
    for e in range(groups):
        live = jnp.where(dest == e, count_ref[0, e], live)
    key = jnp.where(slot - dest * cap < live, slot * columns + column_ref[...], -1)
    key_down = jnp.transpose(jnp.broadcast_to(key, (8, total)))[:, 0:1]
    earlier = lax.broadcasted_iota(jnp.int32, (total, total), 0)
    order = lax.broadcasted_iota(jnp.int32, (total, total), 1)
    same = (key_down == key) & (earlier < order)
    found = jnp.max(jnp.where(same, earlier, -1), axis=0, keepdims=True)
    prev_vmem[...] = jnp.where(found < 0, total, found)
    for i in range(0, slots * columns, total):
        found = jnp.max(jnp.where(key_down == order + i, earlier, -1), axis=0, keepdims=True)
        last_vmem[:, i : i + total] = jnp.where(found < 0, total, found)
    prev_copy = pltpu.make_async_copy(prev_vmem, prev_ref, table_sem.at[0])
    last_copy = pltpu.make_async_copy(last_vmem, last_ref, table_sem.at[1])
    prev_copy.start()
    last_copy.start()
    tile_buf[total] = jnp.zeros((size, size), BF16)
    run_buf[total] = jnp.zeros((size, size), F32)
    w1_top[...] = jnp.zeros(w1_top.shape, BF16)
    w1_low[...] = jnp.zeros(w1_low.shape, BF16)
    for h in range(2):
        w1_top[h * width : h * width + wing, :] = w1_ref[h * wing : (h + 1) * wing, :]
        w1_low[h * width + wing : (h + 1) * width, :] = w1_ref[h * wing : (h + 1) * wing, :]
    prev_copy.wait()
    last_copy.wait()

    def chain(t, c):
        value = tile_buf[t].astype(F32) + run_buf[prev_ref[0, t]]
        run_buf[t] = value
        tile_buf[t] = value.astype(BF16)
        return c

    for i in range(pieces):
        tile_copy(i).wait()
        lax.fori_loop(i * piece, (i + 1) * piece, chain, 0, unroll=4)
        if i == 4:
            gather_start(bank1, 0, 1)
        if i in FORWARD_AT:
            forward(bank1, 0, *FORWARD_AT[i])

    def stage(k, c):
        for s in range(slots):
            for b in range(blocks):
                stage_buf[k, s * size : (s + 1) * size, b * size : (b + 1) * size] = tile_buf[
                    last_ref[0, s * columns + k * blocks + b]
                ]
        return c

    lax.fori_loop(0, n, stage, 0)

    def first_layer(h, origin, fresh):
        packed = bank1[h, origin]
        sources = jnp.concatenate([packed, turn(packed).astype(BF16)], axis=0)
        value = jnp.dot(stage_buf[origin], sources, preferred_element_type=F32)
        if fresh:
            acc1[h] = value
        else:
            acc1[h] += value

    def first_line(h):
        first_layer(h, m, True)

        def step(k, c):
            first_layer(h, line_at(k) * 2 + x, False)
            return c

        lax.fori_loop(1, 4, step, 0)

    def first_across(h, start, stop):
        def step(k, c):
            x_arrival(bank1, 0, h, line_at(k)).wait_recv()
            first_layer(h, line_at(k) * 2 + 1 - x, False)
            return c

        lax.fori_loop(start, stop, step, 0)

    def exchange_first(h):
        keep_left = lax.broadcasted_iota(jnp.int32, (size, width), 1) < wing
        for j in (2, 3, 1, 0):
            at = pl.multiple_of(partner[j] * cap * size, cap * size)
            one = acc1[h, pl.ds(at, size), :]
            two = acc1[h, pl.ds(at + size, size), :]
            part1[h, j] = jnp.where(keep_left, one, pltpu.roll(two, wing, 1)).astype(BF16)
            if j:
                rs1_copy(h, j).start()

    def sum_first(h):
        keep_left = lax.broadcasted_iota(jnp.int32, (size, width), 1) < wing
        row_left = lax.broadcasted_iota(jnp.int32, (1, width), 1) < wing
        for j in range(1, groups):
            rs1_copy(h, j).wait_recv()
        sums = []
        for b in range(blocks):
            value = None
            for j in range(groups):
                hot = hot_ref[0] if j == 0 else got_hot[j]
                weight = jnp.where(row_left, hot[b : b + 1, :], hot[blocks + b : blocks + b + 1, :])
                block = part1[h, 0] if j == 0 else got1[h, j]
                term = weight * block.astype(F32)
                value = term if value is None else value + term
            sums.append(value + pltpu.roll(value, wing, 1))
        for b in range(blocks // 2):
            bank2[h, m, b * size : (b + 1) * size, :] = jnp.where(
                keep_left, sums[b], sums[b + blocks // 2]
            ).astype(BF16)

    forward(bank1, 0, 1, 0)
    first_line(0)
    first_across(0, 0, 2)
    forward(bank1, 0, 1, 1)
    first_across(0, 2, 3)
    forward(bank1, 0, 1, 2)
    first_across(0, 3, 4)
    exchange_first(0)
    first_line(1)
    for j in range(1, groups):
        hot_copy(j).wait_recv()
    sum_first(0)
    gather_start(bank2, 1, 0)
    first_across(1, 0, 4)
    exchange_first(1)
    forward(bank2, 1, 0, 0)
    forward(bank2, 1, 0, 1)
    sum_first(1)
    gather_start(bank2, 1, 1)
    forward(bank2, 1, 0, 2)

    def hidden_of(origin):
        packed = jnp.concatenate([bank2[0, origin], bank2[1, origin]], axis=1)
        parts = []
        for w in (w1_top, w1_low):
            raw = jnp.dot(packed, w[...], preferred_element_type=F32) + b1_ref[...]
            parts.append(jnp.maximum(raw, 0.0).astype(BF16))
        return jnp.concatenate(parts, axis=0)

    def second_layer(origin):
        acc2[...] += jnp.dot(stage_buf[origin], hidden_of(origin), preferred_element_type=F32)

    acc2[...] = jnp.dot(stage_buf[m], hidden_of(m), preferred_element_type=F32)
    for k in range(3):
        forward(bank2, 1, 1, k)

    def second_line(k, c):
        second_layer(line_at(k) * 2 + x)
        return c

    lax.fori_loop(1, 4, second_line, 0)

    def second_across(k, c):
        for h in range(2):
            x_arrival(bank2, 1, h, line_at(k)).wait_recv()
        second_layer(line_at(k) * 2 + 1 - x)
        return c

    lax.fori_loop(0, 3, second_across, 0)
    for h in range(2):
        x_arrival(bank2, 1, h, line_at(3)).wait_recv()
    last = line_at(3) * 2 + 1 - x
    hidden = hidden_of(last)
    for j in (2, 3, 1, 0):
        at = pl.ds(pl.multiple_of(partner[j] * cap * size, cap * size), cap * size)
        value = acc2[at, :] + jnp.dot(stage_buf[last, at, :], hidden, preferred_element_type=F32)
        for r in range(2):
            for c in range(cap):
                part2[r, j, c * half : (c + 1) * half, :] = value[
                    c * size + r * half : c * size + (r + 1) * half, :
                ].astype(BF16)
        if j == 2:
            rs2_copy(0, 2).start()
        elif j == 3:
            rs2_copy(0, 3).start()
            rs2_copy(1, 2).start()
            rs2_copy(1, 3).start()
        elif j == 1:
            rs2_copy(0, 1).start()
            rs2_copy(1, 1).start()

    for i, bank in enumerate((bank1, bank2)):
        for h in range(2):
            gather_drain(bank, i, h)
    for j in range(1, groups):
        hot_copy(j).wait_send()
        for h in range(2):
            rs1_copy(h, j).wait_send()

    for r in range(2):
        for j in (1, 2, 3):
            rs2_copy(r, j).wait_recv()
        sums = []
        for b in range(blocks):
            value = None
            for j in range(groups):
                hot = hot_ref[0] if j == 0 else got_hot[j]
                for c in range(cap):
                    weight = hot[c * blocks + b : c * blocks + b + 1, :]
                    weight = jnp.concatenate([weight] * (w2_ref.shape[0] // width), axis=1)
                    span = slice(c * half, (c + 1) * half)
                    block = part2[r, 0, span, :] if j == 0 else got2[r, j, span, :]
                    term = weight * block.astype(F32)
                    value = term if value is None else value + term
            sums.append(value.astype(BF16))
        raw = jnp.dot(jnp.concatenate(sums, axis=0), w2_ref[...], preferred_element_type=F32)
        raw = (raw + b2_ref[...]).astype(BF16)
        for b in range(blocks):
            out_ref[b * size + r * half : b * size + (r + 1) * half, :] = raw[
                b * half : (b + 1) * half, :
            ]
    for r in range(2):
        for j in (1, 2, 3):
            rs2_copy(r, j).wait_send()


FORWARD_AT = {3: (0, 0), 5: (0, 1), 7: (0, 2)}


def fast_body(
    features,
    edge_tiles,
    tile_slot,
    tile_column,
    mirror_count,
    mirror_block,
    weight_first,
    bias_first,
    weight_second,
    bias_second,
):
    groups = lax.axis_size("group")
    n = lax.axis_size("member")
    total, size, _ = edge_tiles.shape
    rows, width = features.shape
    hidden = weight_first.shape[1]
    outs = weight_second.shape[1]
    blocks = rows // size
    cap = mirror_block.shape[2]
    slots = groups * cap
    columns = n * blocks
    pieces = 8
    fold = rows // 2
    vmem = pl.BlockSpec(memory_space=pltpu.VMEM)
    smem = pl.BlockSpec(memory_space=pltpu.SMEM)
    dma = pltpu.SemaphoreType.DMA
    return pl.pallas_call(
        fast_kernel,
        out_shape=pltpu.VMEM((rows, outs), BF16),
        in_specs=[vmem, vmem, smem, smem, vmem, pl.BlockSpec(memory_space=pl.ANY)] + [vmem] * 4,
        out_specs=vmem,
        scratch_shapes=[
            pltpu.VMEM((total + 1, size, size), BF16),
            pltpu.VMEM((total + 1, size, size), F32),
            pltpu.VMEM((n, slots * size, rows), BF16),
            pltpu.VMEM((2, n, fold, width), BF16),
            pltpu.VMEM((2, n, fold, width), BF16),
            pltpu.VMEM((2, slots * size, width), F32),
            pltpu.VMEM((slots * size, hidden), F32),
            pltpu.VMEM((2, groups, size, width), BF16),
            pltpu.VMEM((2, groups, size, hidden), BF16),
            pltpu.VMEM((2, groups, size, width), BF16),
            pltpu.VMEM((2, groups, size, hidden), BF16),
            pltpu.VMEM((groups, cap * blocks, width), F32),
            pltpu.VMEM((groups, cap * blocks, width), F32),
            pltpu.VMEM((2 * width, hidden), BF16),
            pltpu.VMEM((2 * width, hidden), BF16),
            pltpu.VMEM((1, total), jnp.int32),
            pltpu.VMEM((1, slots * columns), jnp.int32),
            pltpu.SMEM((1, total), jnp.int32),
            pltpu.SMEM((1, slots * columns), jnp.int32),
            dma((2,)),
            dma((pieces,)),
            dma((groups,)),
            dma((groups,)),
            dma((2, 2, 4)),
            dma((2, 2, 4)),
            dma((2, 2, 4)),
            dma((2, 2, 4)),
            dma((2, 2)),
            dma((2, groups)),
            dma((2, groups)),
            dma((2, groups)),
            dma((2, groups)),
        ],
        compiler_params=pltpu.CompilerParams(
            collective_id=1, has_side_effects=True, vmem_limit_bytes=58 * 1024 * 1024
        ),
    )(
        tile_slot,
        tile_column,
        mirror_count,
        jnp.transpose(mirror_block, (0, 2, 1)),
        features,
        edge_tiles,
        weight_first,
        bias_first.reshape(1, -1),
        weight_second,
        bias_second.reshape(1, -1),
    )


def body(features, edge_tiles, tile_slot, tile_column, mirror_count, mirror_block, *weights):
    small = lax.axis_size("member") == 8 and lax.axis_size("group") == 4
    args = (features, edge_tiles, tile_slot, tile_column, mirror_count, mirror_block, *weights)
    return fast_body(*args) if small else general_body(*args)


def solution(mesh):
    placed = (
        P(("group", "member"), None),
        P(("group", "member"), None, None),
        P(("group", "member"), None),
        P(("group", "member"), None),
        P(("group", "member"), None),
        P(("group", "member"), None, None),
        P(),
        P(),
        P(),
        P(),
    )
    return jax.shard_map(
        body, mesh=mesh, in_specs=placed, out_specs=P(("group", "member"), None), check_vma=False
    )
```

```python
import functools

import jax
import jax.numpy as jnp
from jax import lax
from jax.experimental import pallas as pl
from jax.experimental.pallas import tpu as pltpu
from jax.sharding import PartitionSpec as P

F32 = jnp.float32
BF16 = jnp.bfloat16


def general_kernel(
    outer,
    inner,
    groups,
    cap,
    keep,
    slot_ref,
    column_ref,
    count_ref,
    mirror_ref,
    feat_ref,
    tiles_ref,
    w1_ref,
    b1_ref,
    w2_ref,
    b2_ref,
    out_ref,
    tile_buf,
    run_buf,
    stage_buf,
    gather1,
    gather2,
    acc1,
    acc2,
    part1,
    part2,
    got1,
    got2,
    got_hot,
    own_sum,
    hot_ref,
    prev_vmem,
    last_vmem,
    prev_ref,
    last_ref,
    table_sem,
    tile_sem,
    hot_send,
    hot_recv,
    ag1_send,
    ag1_recv,
    rs1_send,
    rs1_recv,
    ag2_send,
    ag2_recv,
    rs2_send,
    rs2_recv,
):
    n = outer * inner
    me = lax.axis_index("member")
    me_outer, me_inner = me // inner, lax.rem(me, inner)
    g = lax.axis_index("group")
    total = tiles_ref.shape[0]
    size = tiles_ref.shape[1]
    rows = feat_ref.shape[0]
    blocks = rows // size
    slots = groups * cap
    columns = n * blocks
    pieces = tile_sem.shape[0]
    piece = total // pieces

    def tile_copy(i):
        span = pl.ds(i * piece, piece)
        return pltpu.make_async_copy(tiles_ref.at[span], tile_buf.at[span], tile_sem.at[i])

    def outer_copy(src, bank, j, send, recv, arriving=False):
        from_outer = lax.rem(me_outer + outer - j, outer)
        origin = from_outer * inner + me_inner
        to = lax.rem(me_outer + j, outer) * inner + me_inner
        return pltpu.make_async_remote_copy(
            src_ref=src,
            dst_ref=bank.at[origin if arriving else me],
            send_sem=send.at[j],
            recv_sem=recv.at[j],
            device_id={"member": to},
            device_id_type=pl.DeviceIdType.MESH,
        )

    def inner_copy(src, bank, j, hop, send, recv, arriving=False):
        from_outer = lax.rem(me_outer + outer - j, outer)
        from_inner = lax.rem(me_inner + inner - hop, inner)
        mine = from_outer * inner + me_inner
        origin = from_outer * inner + from_inner
        to = me_outer * inner + lax.rem(me_inner + hop, inner)
        at = outer + j * (inner - 1) + hop - 1
        return pltpu.make_async_remote_copy(
            src_ref=src if j == 0 else bank.at[mine],
            dst_ref=bank.at[origin if arriving else mine],
            send_sem=send.at[at],
            recv_sem=recv.at[at],
            device_id={"member": to},
            device_id_type=pl.DeviceIdType.MESH,
        )

    hops = sorted(range(1, outer), key=lambda j: (min(j, outer - j), j))

    def over_inner(do):
        def step(hop, c):
            do(hop)
            return c

        lax.fori_loop(1, inner, step, 0)

    def gather_start(src, bank, send, recv):
        over_inner(lambda hop: inner_copy(src, bank, 0, hop, send, recv).start())
        for j in hops:
            outer_copy(src, bank, j, send, recv).start()

    def forward(src, bank, j, send, recv):
        outer_copy(src, bank, j, send, recv, True).wait_recv()
        over_inner(lambda hop: inner_copy(src, bank, j, hop, send, recv).start())

    def gather_inner(src, bank, j, send, recv, use):
        def do(hop):
            inner_copy(src, bank, j, hop, send, recv, True).wait_recv()
            from_outer = lax.rem(me_outer + outer - j, outer)
            use(from_outer * inner + lax.rem(me_inner + inner - hop, inner))

        over_inner(do)

    def outer_origin(j):
        return lax.rem(me_outer + outer - j, outer) * inner + me_inner

    def gather_drain(src, bank, send, recv):
        for j in hops:
            outer_copy(src, bank, j, send, recv).wait_send()
        for j in range(outer):
            over_inner(lambda hop: inner_copy(src, bank, j, hop, send, recv).wait_send())

    def group_copy(bank, got, k, send, recv):
        to = lax.rem(g + k, groups)
        return pltpu.make_async_remote_copy(
            src_ref=bank.at[to],
            dst_ref=got.at[k],
            send_sem=send.at[k],
            recv_sem=recv.at[k],
            device_id={"group": to},
            device_id_type=pl.DeviceIdType.MESH,
        )

    for i in range(pieces):
        tile_copy(i).start()

    barrier = pltpu.get_barrier_semaphore()

    def greet_member(k, c):
        pl.semaphore_signal(
            barrier,
            inc=1,
            device_id={"member": lax.rem(me + k, n)},
            device_id_type=pl.DeviceIdType.MESH,
        )
        return c

    lax.fori_loop(1, n, greet_member, 0)
    for k in range(1, groups):
        pl.semaphore_signal(
            barrier,
            inc=1,
            device_id={"group": lax.rem(g + k, groups)},
            device_id_type=pl.DeviceIdType.MESH,
        )
    pl.semaphore_wait(barrier, n - 1 + groups - 1)

    ag1 = (feat_ref, gather1)
    sem1 = (ag1_send, ag1_recv)
    gather_start(*ag1, *sem1)

    for e in range(groups):
        shape = (cap * blocks, feat_ref.shape[1])
        line = lax.broadcasted_iota(jnp.int32, shape, 0)
        value = jnp.zeros(shape, F32)
        for c in range(cap):
            target = jnp.where(c < count_ref[0, e], c * blocks + mirror_ref[0, e, c], -1)
            value = jnp.where(line == target, 1.0, value)
        hot_ref[e] = value
    for k in range(1, groups):
        group_copy(hot_ref, got_hot, k, hot_send, hot_recv).start()

    slot = slot_ref[...]
    dest = slot // cap
    live = jnp.zeros(slot.shape, jnp.int32)
    for e in range(groups):
        live = jnp.where(dest == e, count_ref[0, e], live)
    key = jnp.where(slot - dest * cap < live, slot * columns + column_ref[...], -1)
    key_down = jnp.transpose(jnp.broadcast_to(key, (8, total)))[:, 0:1]
    earlier = lax.broadcasted_iota(jnp.int32, (total, total), 0)
    order = lax.broadcasted_iota(jnp.int32, (total, total), 1)
    same = (key_down == key) & (earlier < order)
    found = jnp.max(jnp.where(same, earlier, -1), axis=0, keepdims=True)
    prev_vmem[...] = jnp.where(found < 0, total, found)
    for i in range(0, slots * columns, total):
        found = jnp.max(
            jnp.where(key_down == order + i, earlier, -1), axis=0, keepdims=True
        )
        last_vmem[:, i : i + total] = jnp.where(found < 0, total, found)
    prev_copy = pltpu.make_async_copy(prev_vmem, prev_ref, table_sem.at[0])
    last_copy = pltpu.make_async_copy(last_vmem, last_ref, table_sem.at[1])
    prev_copy.start()
    last_copy.start()
    tile_buf[total] = jnp.zeros((size, size), BF16)
    run_buf[total] = jnp.zeros((size, size), F32)

    prev_copy.wait()
    last_copy.wait()

    def chain(t, c):
        value = tile_buf[t].astype(F32) + run_buf[prev_ref[0, t]]
        run_buf[t] = value
        tile_buf[t] = value.astype(BF16)
        return c

    for i in range(pieces):
        tile_copy(i).wait()
        lax.fori_loop(i * piece, (i + 1) * piece, chain, 0, unroll=4)
        if i % 2 == 1 and i // 2 < len(hops):
            forward(*ag1, hops[i // 2], *sem1)
    for j in hops[pieces // 2 :]:
        forward(*ag1, j, *sem1)

    def stage(origin, at):
        for s in range(slots):
            for b in range(blocks):
                stage_buf[at, s * size : (s + 1) * size, b * size : (b + 1) * size] = tile_buf[
                    last_ref[0, s * columns + origin * blocks + b]
                ]

    if keep:

        def stage_all(k, c):
            stage(k, k)
            return c

        lax.fori_loop(0, n, stage_all, 0)

    def place(origin):
        if keep:
            return origin
        stage(origin, 0)
        return 0

    def combine(part, got):
        sums = []
        for b in range(blocks):
            value = None
            for k in range(groups):
                hot = hot_ref[g] if k == 0 else got_hot[k]
                for c in range(cap):
                    block = (
                        part[g, c * size : (c + 1) * size, :]
                        if k == 0
                        else got[k, c * size : (c + 1) * size, :]
                    )
                    weight = hot[c * blocks + b : c * blocks + b + 1, :]
                    repeat = block.shape[1] // weight.shape[1]
                    if repeat > 1:
                        weight = jnp.concatenate([weight] * repeat, axis=1)
                    term = weight * block.astype(F32)
                    value = term if value is None else value + term
            sums.append(value.astype(BF16))
        return sums

    acc1[...] = jnp.dot(stage_buf[place(me)], feat_ref[...], preferred_element_type=F32)

    def first_layer(origin):
        at = place(origin)
        acc1[...] += jnp.dot(stage_buf[at], gather1[origin], preferred_element_type=F32)

    for j in hops:
        first_layer(outer_origin(j))
    for j in [0] + hops:
        gather_inner(*ag1, j, *sem1, first_layer)
    for e in range(groups):
        part1[e] = acc1[e * cap * size : (e + 1) * cap * size, :].astype(BF16)
    for k in range(1, groups):
        group_copy(part1, got1, k, rs1_send, rs1_recv).start()
    for k in range(1, groups):
        group_copy(hot_ref, got_hot, k, hot_send, hot_recv).wait_recv()
    for k in range(1, groups):
        group_copy(part1, got1, k, rs1_send, rs1_recv).wait_recv()
    sums = combine(part1, got1)
    for b in range(blocks):
        own_sum[b * size : (b + 1) * size, :] = sums[b]

    ag2 = (own_sum, gather2)
    sem2 = (ag2_send, ag2_recv)
    gather_start(*ag2, *sem2)

    def hidden_of(value):
        raw = jnp.dot(value, w1_ref[...], preferred_element_type=F32) + b1_ref[...]
        return jnp.maximum(raw, 0.0).astype(BF16)

    acc2[...] = jnp.dot(stage_buf[place(me)], hidden_of(own_sum[...]), preferred_element_type=F32)

    def second_layer(origin):
        at = place(origin)
        acc2[...] += jnp.dot(
            stage_buf[at], hidden_of(gather2[origin]), preferred_element_type=F32
        )

    waiting = []
    for j in hops:
        forward(*ag2, j, *sem2)
        for i in waiting:
            second_layer(outer_origin(i))
        waiting = [j]
        if j == hops[1]:
            gather_inner(*ag2, 0, *sem2, second_layer)
    for i in waiting:
        second_layer(outer_origin(i))
    for j in hops:
        gather_inner(*ag2, j, *sem2, second_layer)
    for e in range(groups):
        part2[e] = acc2[e * cap * size : (e + 1) * cap * size, :].astype(BF16)
    for k in range(1, groups):
        group_copy(part2, got2, k, rs2_send, rs2_recv).start()

    gather_drain(*ag1, *sem1)
    gather_drain(*ag2, *sem2)
    for k in range(1, groups):
        group_copy(hot_ref, got_hot, k, hot_send, hot_recv).wait_send()
        group_copy(part1, got1, k, rs1_send, rs1_recv).wait_send()
    for k in range(1, groups):
        group_copy(part2, got2, k, rs2_send, rs2_recv).wait_recv()
    sums = combine(part2, got2)
    for b in range(blocks):
        raw = jnp.dot(sums[b], w2_ref[...], preferred_element_type=F32) + b2_ref[...]
        out_ref[b * size : (b + 1) * size, :] = raw.astype(BF16)
    for k in range(1, groups):
        group_copy(part2, got2, k, rs2_send, rs2_recv).wait_send()


def general_body(
    features,
    edge_tiles,
    tile_slot,
    tile_column,
    mirror_count,
    mirror_block,
    weight_first,
    bias_first,
    weight_second,
    bias_second,
):
    groups = lax.axis_size("group")
    n = lax.axis_size("member")
    total, size, _ = edge_tiles.shape
    rows, width = features.shape
    hidden = weight_first.shape[1]
    outs = weight_second.shape[1]
    blocks = rows // size
    cap = mirror_block.shape[2]
    slots = groups * cap
    columns = n * blocks
    keep = slots * columns <= 2 * total
    pieces = 8 if total % 8 == 0 else 1
    outer = 4
    inner = n // outer
    vmem = pl.BlockSpec(memory_space=pltpu.VMEM)
    smem = pl.BlockSpec(memory_space=pltpu.SMEM)
    dma = pltpu.SemaphoreType.DMA
    return pl.pallas_call(
        functools.partial(general_kernel, outer, inner, groups, cap, keep),
        out_shape=jax.ShapeDtypeStruct((rows, outs), BF16),
        in_specs=[vmem, vmem, smem, smem, vmem, pl.BlockSpec(memory_space=pl.ANY)] + [vmem] * 4,
        out_specs=vmem,
        scratch_shapes=[
            pltpu.VMEM((total + 1, size, size), BF16),
            pltpu.VMEM((total + 1, size, size), F32),
            pltpu.VMEM((n if keep else 1, slots * size, rows), BF16),
            pltpu.VMEM((n, rows, width), BF16),
            pltpu.VMEM((n, rows, width), BF16),
            pltpu.VMEM((slots * size, width), F32),
            pltpu.VMEM((slots * size, hidden), F32),
            pltpu.VMEM((groups, cap * size, width), BF16),
            pltpu.VMEM((groups, cap * size, hidden), BF16),
            pltpu.VMEM((groups, cap * size, width), BF16),
            pltpu.VMEM((groups, cap * size, hidden), BF16),
            pltpu.VMEM((groups, cap * blocks, width), F32),
            pltpu.VMEM((rows, width), BF16),
            pltpu.VMEM((groups, cap * blocks, width), F32),
            pltpu.VMEM((1, total), jnp.int32),
            pltpu.VMEM((1, slots * columns), jnp.int32),
            pltpu.SMEM((1, total), jnp.int32),
            pltpu.SMEM((1, slots * columns), jnp.int32),
            dma((2,)),
            dma((pieces,)),
            dma((groups,)),
            dma((groups,)),
            dma((n,)),
            dma((n,)),
            dma((groups,)),
            dma((groups,)),
            dma((n,)),
            dma((n,)),
            dma((groups,)),
            dma((groups,)),
        ],
        compiler_params=pltpu.CompilerParams(
            collective_id=0, has_side_effects=True, vmem_limit_bytes=56 * 1024 * 1024
        ),
    )(
        tile_slot,
        tile_column,
        mirror_count,
        mirror_block,
        features,
        edge_tiles,
        weight_first,
        bias_first.reshape(1, -1),
        weight_second,
        bias_second.reshape(1, -1),
    )


def fast_kernel(
    slot_ref,
    column_ref,
    count_ref,
    mirror_ref,
    feat_ref,
    tiles_ref,
    w1_ref,
    b1_ref,
    w2_ref,
    b2_ref,
    out_ref,
    tile_buf,
    run_buf,
    stage_buf,
    bank1,
    bank2,
    acc1,
    acc2,
    part1,
    part2,
    got1,
    got2,
    got_hot,
    hot_ref,
    w1_top,
    w1_low,
    prev_vmem,
    last_vmem,
    prev_ref,
    last_ref,
    table_sem,
    tile_sem,
    hot_send,
    hot_recv,
    z_send,
    z_recv,
    x_send,
    x_recv,
    f_send,
    rs1_send,
    rs1_recv,
    rs2_send,
    rs2_recv,
):
    groups, cap, n = 4, 2, 8
    m = lax.axis_index("member")
    g = lax.axis_index("group")
    z, x = m // 2, lax.rem(m, 2)
    total, size = tiles_ref.shape[0], tiles_ref.shape[1]
    rows, width = feat_ref.shape
    blocks = rows // size
    slots = groups * cap
    columns = n * blocks
    pieces = tile_sem.shape[0]
    piece = total // pieces
    wing, fold = width // 2, rows // 2
    half = size // 2

    low = 1 - z // 2
    near = z + 1 - 2 * lax.rem(z, 2)
    line = [near, 1 + low, 3 * low]
    mid = lax.rem(z, 3) > 0
    partner = [g, g + 1 - 2 * lax.rem(g, 2), lax.rem(g + 2, groups), groups - 1 - g]

    def line_at(k):
        hi, lo = k // 2, lax.rem(k, 2)
        return (1 - hi) * ((1 - lo) * z + lo * line[0]) + hi * ((1 - lo) * line[1] + lo * line[2])

    def tile_copy(i):
        span = pl.ds(i * piece, piece)
        return pltpu.make_async_copy(tiles_ref.at[span], tile_buf.at[span], tile_sem.at[i])

    def to_member(bank, i, h, at, send, recv, device):
        block = bank.at[h, at]
        return pltpu.make_async_remote_copy(
            src_ref=block,
            dst_ref=block,
            send_sem=send,
            recv_sem=recv,
            device_id={"member": device},
            device_id_type=pl.DeviceIdType.MESH,
        )

    def z_copy(bank, i, h, to):
        return to_member(bank, i, h, m, z_send.at[i, h, to], z_recv.at[i, h, z], to * 2 + x)

    def z_arrival(bank, i, h, origin):
        return to_member(
            bank, i, h, origin * 2 + x, z_send.at[i, h, origin], z_recv.at[i, h, origin], origin * 2 + x
        )

    def far_copy(bank, i, h):
        return to_member(
            bank, i, h, line[2] * 2 + x, f_send.at[i, h], z_recv.at[i, h, line[2]], near * 2 + x
        )

    def x_copy(bank, i, h, origin):
        return to_member(
            bank, i, h, origin * 2 + x, x_send.at[i, h, origin], x_recv.at[i, h, origin], z * 2 + 1 - x
        )

    def x_arrival(bank, i, h, origin):
        return to_member(
            bank, i, h, origin * 2 + 1 - x, x_send.at[i, h, origin], x_recv.at[i, h, origin], z * 2 + 1 - x
        )

    def gather_start(bank, i, h):
        x_copy(bank, i, h, z).start()
        z_copy(bank, i, h, line[0]).start()
        z_copy(bank, i, h, line[1]).start()
        z_copy(bank, i, h, line[2]).start()

    def forward(bank, i, h, k):
        z_arrival(bank, i, h, line[k]).wait_recv()
        x_copy(bank, i, h, line[k]).start()

    def gather_drain(bank, i, h):
        z_copy(bank, i, h, line[0]).wait_send()
        z_copy(bank, i, h, line[1]).wait_send()
        z_copy(bank, i, h, line[2]).wait_send()

        for k in range(4):
            x_copy(bank, i, h, (z, *line)[k]).wait_send()

    def group_copy(src, dst, j, send, recv):
        return pltpu.make_async_remote_copy(
            src_ref=src,
            dst_ref=dst,
            send_sem=send,
            recv_sem=recv,
            device_id={"group": partner[j]},
            device_id_type=pl.DeviceIdType.MESH,
        )

    def hot_copy(j):
        return group_copy(hot_ref.at[j], got_hot.at[j], j, hot_send.at[j], hot_recv.at[j])

    def rs1_copy(h, j):
        return group_copy(part1.at[h, j], got1.at[h, j], j, rs1_send.at[h, j], rs1_recv.at[h, j])

    def rs2_copy(r, j):
        return group_copy(part2.at[r, j], got2.at[r, j], j, rs2_send.at[r, j], rs2_recv.at[r, j])

    for i in range(pieces):
        tile_copy(i).start()

    barrier = pltpu.get_barrier_semaphore()

    def greet_member(k, c):
        pl.semaphore_signal(
            barrier,
            inc=1,
            device_id={"member": lax.rem(m + k, n)},
            device_id_type=pl.DeviceIdType.MESH,
        )
        return c

    lax.fori_loop(1, n, greet_member, 0)
    for j in range(1, groups):
        pl.semaphore_signal(
            barrier,
            inc=1,
            device_id={"group": partner[j]},
            device_id_type=pl.DeviceIdType.MESH,
        )

    def turn(value):
        return pltpu.roll(value.astype(F32), wing, 1)

    lane = lax.broadcasted_iota(jnp.int32, (fold, width), 1)
    left = lane < wing
    for h in range(2):
        top, bottom = feat_ref[0:fold, :].astype(F32), feat_ref[fold:rows, :].astype(F32)
        packed = jnp.where(left, top, turn(bottom)) if h == 0 else jnp.where(left, turn(top), bottom)
        bank1[h, m] = packed.astype(BF16)

    for j in range(groups):
        shape = (cap * blocks, width)
        row = lax.broadcasted_iota(jnp.int32, shape, 0)
        value = jnp.zeros(shape, F32)
        for c in range(cap):
            e = partner[j]
            target = jnp.where(c < count_ref[0, e], c * blocks + mirror_ref[0, c, e], -1)
            value = jnp.where(row == target, 1.0, value)
        hot_ref[j] = value

    pl.semaphore_wait(barrier, n - 1 + groups - 1)

    gather_start(bank1, 0, 0)
    for j in range(1, groups):
        hot_copy(j).start()

    slot = slot_ref[...]
    dest = slot // cap
    live = jnp.zeros(slot.shape, jnp.int32)
    for e in range(groups):
        live = jnp.where(dest == e, count_ref[0, e], live)
    key = jnp.where(slot - dest * cap < live, slot * columns + column_ref[...], -1)
    key_down = jnp.transpose(jnp.broadcast_to(key, (8, total)))[:, 0:1]
    earlier = lax.broadcasted_iota(jnp.int32, (total, total), 0)
    order = lax.broadcasted_iota(jnp.int32, (total, total), 1)
    same = (key_down == key) & (earlier < order)
    found = jnp.max(jnp.where(same, earlier, -1), axis=0, keepdims=True)
    prev_vmem[...] = jnp.where(found < 0, total, found)
    for i in range(0, slots * columns, total):
        found = jnp.max(jnp.where(key_down == order + i, earlier, -1), axis=0, keepdims=True)
        last_vmem[:, i : i + total] = jnp.where(found < 0, total, found)
    prev_copy = pltpu.make_async_copy(prev_vmem, prev_ref, table_sem.at[0])
    last_copy = pltpu.make_async_copy(last_vmem, last_ref, table_sem.at[1])
    prev_copy.start()
    last_copy.start()
    tile_buf[total] = jnp.zeros((size, size), BF16)
    run_buf[total] = jnp.zeros((size, size), F32)
    w1_top[...] = jnp.zeros(w1_top.shape, BF16)
    w1_low[...] = jnp.zeros(w1_low.shape, BF16)
    for h in range(2):
        w1_top[h * width : h * width + wing, :] = w1_ref[h * wing : (h + 1) * wing, :]
        w1_low[h * width + wing : (h + 1) * width, :] = w1_ref[h * wing : (h + 1) * wing, :]
    prev_copy.wait()
    last_copy.wait()

    def chain(t, c):
        value = tile_buf[t].astype(F32) + run_buf[prev_ref[0, t]]
        run_buf[t] = value
        tile_buf[t] = value.astype(BF16)
        return c

    for i in range(pieces):
        tile_copy(i).wait()
        lax.fori_loop(i * piece, (i + 1) * piece, chain, 0, unroll=4)
        if i == 4:
            gather_start(bank1, 0, 1)
        if i in FORWARD_AT:
            forward(bank1, 0, *FORWARD_AT[i])

    def stage(k, c):
        for s in range(slots):
            for b in range(blocks):
                stage_buf[k, s * size : (s + 1) * size, b * size : (b + 1) * size] = tile_buf[
                    last_ref[0, s * columns + k * blocks + b]
                ]
        return c

    lax.fori_loop(0, n, stage, 0)

    def first_layer(h, origin, fresh):
        packed = bank1[h, origin]
        sources = jnp.concatenate([packed, turn(packed).astype(BF16)], axis=0)
        value = jnp.dot(stage_buf[origin], sources, preferred_element_type=F32)
        if fresh:
            acc1[h] = value
        else:
            acc1[h] += value

    def first_line(h):
        first_layer(h, m, True)

        def step(k, c):
            first_layer(h, line_at(k) * 2 + x, False)
            return c

        lax.fori_loop(1, 4, step, 0)

    def first_across(h, start, stop):
        def step(k, c):
            x_arrival(bank1, 0, h, line_at(k)).wait_recv()
            first_layer(h, line_at(k) * 2 + 1 - x, False)
            return c

        lax.fori_loop(start, stop, step, 0)

    def exchange_first(h):
        keep_left = lax.broadcasted_iota(jnp.int32, (size, width), 1) < wing
        for j in (2, 3, 1, 0):
            at = pl.multiple_of(partner[j] * cap * size, cap * size)
            one = acc1[h, pl.ds(at, size), :]
            two = acc1[h, pl.ds(at + size, size), :]
            part1[h, j] = jnp.where(keep_left, one, pltpu.roll(two, wing, 1)).astype(BF16)
            if j:
                rs1_copy(h, j).start()

    def sum_first(h):
        keep_left = lax.broadcasted_iota(jnp.int32, (size, width), 1) < wing
        row_left = lax.broadcasted_iota(jnp.int32, (1, width), 1) < wing
        for j in range(1, groups):
            rs1_copy(h, j).wait_recv()
        sums = []
        for b in range(blocks):
            value = None
            for j in range(groups):
                hot = hot_ref[0] if j == 0 else got_hot[j]
                weight = jnp.where(row_left, hot[b : b + 1, :], hot[blocks + b : blocks + b + 1, :])
                block = part1[h, 0] if j == 0 else got1[h, j]
                term = weight * block.astype(F32)
                value = term if value is None else value + term
            sums.append(value + pltpu.roll(value, wing, 1))
        for b in range(blocks // 2):
            bank2[h, m, b * size : (b + 1) * size, :] = jnp.where(
                keep_left, sums[b], sums[b + blocks // 2]
            ).astype(BF16)

    forward(bank1, 0, 1, 0)
    first_line(0)
    first_across(0, 0, 2)
    forward(bank1, 0, 1, 1)
    first_across(0, 2, 4)
    exchange_first(0)
    forward(bank1, 0, 1, 2)
    first_line(1)
    for j in range(1, groups):
        hot_copy(j).wait_recv()
    sum_first(0)
    gather_start(bank2, 1, 0)
    first_across(1, 0, 4)
    exchange_first(1)
    forward(bank2, 1, 0, 0)
    forward(bank2, 1, 0, 1)
    sum_first(1)
    gather_start(bank2, 1, 1)
    forward(bank2, 1, 0, 2)

    def hidden_of(origin):
        packed = jnp.concatenate([bank2[0, origin], bank2[1, origin]], axis=1)
        parts = []
        for w in (w1_top, w1_low):
            raw = jnp.dot(packed, w[...], preferred_element_type=F32) + b1_ref[...]
            parts.append(jnp.maximum(raw, 0.0).astype(BF16))
        return jnp.concatenate(parts, axis=0)

    def second_layer(origin):
        acc2[...] += jnp.dot(stage_buf[origin], hidden_of(origin), preferred_element_type=F32)

    acc2[...] = jnp.dot(stage_buf[m], hidden_of(m), preferred_element_type=F32)
    for k in range(3):
        forward(bank2, 1, 1, k)
        second_layer(line[k] * 2 + x)

    def second_across(k, c):
        for h in range(2):
            x_arrival(bank2, 1, h, line_at(k)).wait_recv()
        second_layer(line_at(k) * 2 + 1 - x)
        return c

    lax.fori_loop(0, 3, second_across, 0)
    for h in range(2):
        x_arrival(bank2, 1, h, line_at(3)).wait_recv()
    last = line_at(3) * 2 + 1 - x
    hidden = hidden_of(last)
    for j in (2, 3, 1, 0):
        at = pl.ds(pl.multiple_of(partner[j] * cap * size, cap * size), cap * size)
        value = acc2[at, :] + jnp.dot(stage_buf[last, at, :], hidden, preferred_element_type=F32)
        for r in range(2):
            for c in range(cap):
                part2[r, j, c * half : (c + 1) * half, :] = value[
                    c * size + r * half : c * size + (r + 1) * half, :
                ].astype(BF16)
        if j == 2:
            rs2_copy(0, 2).start()
        elif j == 3:
            rs2_copy(0, 3).start()
            rs2_copy(1, 2).start()
            rs2_copy(1, 3).start()
        elif j == 1:
            rs2_copy(0, 1).start()
            rs2_copy(1, 1).start()

    for i, bank in enumerate((bank1, bank2)):
        for h in range(2):
            gather_drain(bank, i, h)
    for j in range(1, groups):
        hot_copy(j).wait_send()
        for h in range(2):
            rs1_copy(h, j).wait_send()

    for r in range(2):
        for j in (1, 2, 3):
            rs2_copy(r, j).wait_recv()
        sums = []
        for b in range(blocks):
            value = None
            for j in range(groups):
                hot = hot_ref[0] if j == 0 else got_hot[j]
                for c in range(cap):
                    weight = hot[c * blocks + b : c * blocks + b + 1, :]
                    weight = jnp.concatenate([weight] * (w2_ref.shape[0] // width), axis=1)
                    span = slice(c * half, (c + 1) * half)
                    block = part2[r, 0, span, :] if j == 0 else got2[r, j, span, :]
                    term = weight * block.astype(F32)
                    value = term if value is None else value + term
            sums.append(value.astype(BF16))
        raw = jnp.dot(jnp.concatenate(sums, axis=0), w2_ref[...], preferred_element_type=F32)
        raw = (raw + b2_ref[...]).astype(BF16)
        for b in range(blocks):
            out_ref[b * size + r * half : b * size + (r + 1) * half, :] = raw[
                b * half : (b + 1) * half, :
            ]
    for r in range(2):
        for j in (1, 2, 3):
            rs2_copy(r, j).wait_send()


FORWARD_AT = {3: (0, 0), 5: (0, 1), 7: (0, 2)}


def fast_body(
    features,
    edge_tiles,
    tile_slot,
    tile_column,
    mirror_count,
    mirror_block,
    weight_first,
    bias_first,
    weight_second,
    bias_second,
):
    groups = lax.axis_size("group")
    n = lax.axis_size("member")
    total, size, _ = edge_tiles.shape
    rows, width = features.shape
    hidden = weight_first.shape[1]
    outs = weight_second.shape[1]
    blocks = rows // size
    cap = mirror_block.shape[2]
    slots = groups * cap
    columns = n * blocks
    pieces = 8
    fold = rows // 2
    vmem = pl.BlockSpec(memory_space=pltpu.VMEM)
    smem = pl.BlockSpec(memory_space=pltpu.SMEM)
    dma = pltpu.SemaphoreType.DMA
    return pl.pallas_call(
        fast_kernel,
        out_shape=pltpu.VMEM((rows, outs), BF16),
        in_specs=[vmem, vmem, smem, smem, vmem, pl.BlockSpec(memory_space=pl.ANY)] + [vmem] * 4,
        out_specs=vmem,
        scratch_shapes=[
            pltpu.VMEM((total + 1, size, size), BF16),
            pltpu.VMEM((total + 1, size, size), F32),
            pltpu.VMEM((n, slots * size, rows), BF16),
            pltpu.VMEM((2, n, fold, width), BF16),
            pltpu.VMEM((2, n, fold, width), BF16),
            pltpu.VMEM((2, slots * size, width), F32),
            pltpu.VMEM((slots * size, hidden), F32),
            pltpu.VMEM((2, groups, size, width), BF16),
            pltpu.VMEM((2, groups, size, hidden), BF16),
            pltpu.VMEM((2, groups, size, width), BF16),
            pltpu.VMEM((2, groups, size, hidden), BF16),
            pltpu.VMEM((groups, cap * blocks, width), F32),
            pltpu.VMEM((groups, cap * blocks, width), F32),
            pltpu.VMEM((2 * width, hidden), BF16),
            pltpu.VMEM((2 * width, hidden), BF16),
            pltpu.VMEM((1, total), jnp.int32),
            pltpu.VMEM((1, slots * columns), jnp.int32),
            pltpu.SMEM((1, total), jnp.int32),
            pltpu.SMEM((1, slots * columns), jnp.int32),
            dma((2,)),
            dma((pieces,)),
            dma((groups,)),
            dma((groups,)),
            dma((2, 2, 4)),
            dma((2, 2, 4)),
            dma((2, 2, 4)),
            dma((2, 2, 4)),
            dma((2, 2)),
            dma((2, groups)),
            dma((2, groups)),
            dma((2, groups)),
            dma((2, groups)),
        ],
        compiler_params=pltpu.CompilerParams(
            collective_id=1, has_side_effects=True, vmem_limit_bytes=58 * 1024 * 1024
        ),
    )(
        tile_slot,
        tile_column,
        mirror_count,
        jnp.transpose(mirror_block, (0, 2, 1)),
        features,
        edge_tiles,
        weight_first,
        bias_first.reshape(1, -1),
        weight_second,
        bias_second.reshape(1, -1),
    )


def body(features, edge_tiles, tile_slot, tile_column, mirror_count, mirror_block, *weights):
    small = lax.axis_size("member") == 8 and lax.axis_size("group") == 4
    args = (features, edge_tiles, tile_slot, tile_column, mirror_count, mirror_block, *weights)
    return fast_body(*args) if small else general_body(*args)


def solution(mesh):
    placed = (
        P(("group", "member"), None),
        P(("group", "member"), None, None),
        P(("group", "member"), None),
        P(("group", "member"), None),
        P(("group", "member"), None),
        P(("group", "member"), None, None),
        P(),
        P(),
        P(),
        P(),
    )
    return jax.shard_map(
        body, mesh=mesh, in_specs=placed, out_specs=P(("group", "member"), None), check_vma=False
    )
```
